512 devices in a mesh: gx: 32 (over z_hi, y, core), gz: 16 (over z_lo, x).
Axes of the slice: x: 4, y: 8, z: 8 (z_hi: 2, z_lo: 4; z = z_hi * 4 + z_lo), core: 2. Of those that a mesh axis runs over, the one named last changes fastest.
Arguments:
- velocity: float32 [3, 2, 6144, 4096], P(None, None, 'gz', 'gx'), may hold values from -6 to 6
- metric_index: int32 [4096], P('gx'), may hold values from 0 to 63
- jac_table: float32 [64], replicated, may hold values from 0.5 to 2
- bend_table: float32 [64], replicated, may hold values from -1 to 1
Outputs:
- first_derivative: float32 [3, 2, 6144, 4096], P(None, None, 'gz', 'gx')
- second_derivative: float32 [3, 2, 6144, 4096], P(None, None, 'gz', 'gx')
- plane_energy: float32 [3, 2], replicated
The draws below stay inside these ranges and needn't reach their ends.
Inputs may be any that keep to these rules, and one draw needn't show every extreme that they name: `metric_index`: each entry names a row of the metric tables.
All inputs are finite; a program needn't handle non-finite values.
Results may differ from the reference program's by a relative error of at most 0.00007.
Values sent between devices are 32-bit elements; how exact they have to be, the bound alone decides.
A program may use at most 64 MiB of HBM per device.

```python
import math
import jax
import jax.numpy as jnp
from jax import lax

YW = 2
TABLE = 64
NX = 4096
NZ = 6144


def plant(array, stream_key, low, high):
    extent = array.shape
    index_at = [jax.random.randint(jax.random.fold_in(stream_key, axis), (), 0, extent[axis]) for axis in range(len(extent))]
    array = array.at[tuple(index_at)].set(low)
    longest = extent.index(max(extent))
    index_at[longest] = (index_at[longest] + 1) % extent[longest]
    return array.at[tuple(index_at)].set(high)


def block_scale(key, dims, cuts, smallest, high):
    def one(position, blocks):
        heights = jax.random.uniform(jax.random.fold_in(jax.random.fold_in(key, 6), position), (blocks,), jnp.float32, smallest / len(cuts), high / len(cuts))
        return jnp.repeat(jnp.exp(heights), dims[position] // blocks).reshape((-1,) + (1,) * (len(dims) - position - 1))

    level = one(*cuts[0])
    for cut in cuts[1:]:
        level = level * one(*cut)
    return level


def gaussian(stream_key, shape, width, most, pieces=(), held_as=jnp.bfloat16):
    entries = jax.random.normal(stream_key, shape, jnp.float32) * width
    if len(pieces) > 0:
        entries = block_scale(stream_key, shape, pieces, -0.22, 0.18) * entries
    return jnp.clip(entries, min=-most, max=most).astype(held_as)


def setup_inputs(seed: int = 0) -> dict:
    streams_of = jax.random.split(jax.random.key(seed), 5)
    return {
        "velocity": gaussian(streams_of[0], (3, YW, NZ, NX), 1.0, 6.0, ((2, 16), (3, 32)), jnp.float32),
        "metric_index": plant(jax.random.randint(streams_of[1], (NX,), 0, TABLE), jax.random.fold_in(streams_of[1], 1), 0, TABLE - 1).astype(jnp.int32),
        "jac_table": jnp.clip(jnp.exp(jax.random.uniform(streams_of[2], (TABLE,), jnp.float32, math.log(0.5), math.log(2.0))), 0.5, 2.0),
        "bend_table": jnp.clip(jax.random.uniform(streams_of[3], (TABLE,), jnp.float32, -1.0, 1.0), -1.0, 1.0),
    }


def spectral(field):
    count = field.shape[-1]
    modes = jnp.fft.rfft(field, axis=-1)
    theta = 2.0 * math.pi * jnp.arange(count // 2 + 1) / count
    first_sym = ((14.0 / 9.0) * jnp.sin(theta) + (1.0 / 18.0) * jnp.sin(2.0 * theta)) / (1.0 + (2.0 / 3.0) * jnp.cos(theta))
    second_sym = -(2.0 * (12.0 / 11.0) * (1.0 - jnp.cos(theta)) + (3.0 / 22.0) * (1.0 - jnp.cos(2.0 * theta))) / (1.0 + (4.0 / 11.0) * jnp.cos(theta))
    first_xi = jnp.fft.irfft(1j * first_sym * modes, n=count, axis=-1).astype(field.dtype)
    second_xi = jnp.fft.irfft(second_sym * modes, n=count, axis=-1).astype(field.dtype)
    return first_xi, second_xi


def reference(velocity, metric_index, jac_table, bend_table):
    first_xi, second_xi = lax.map(spectral, velocity)
    jac = jac_table[metric_index]
    bend = bend_table[metric_index]
    first = first_xi / jac
    second = (second_xi - bend * first) / (jac * jac)
    energy = jnp.mean(first * first, axis=(2, 3))
    return first, second, energy
```

```python
import functools

import jax
import jax.numpy as jnp
import numpy as np
from jax import lax
from jax.experimental import pallas as pl
from jax.experimental.pallas import tpu as pltpu
from jax.sharding import PartitionSpec as P


MESH = pl.DeviceIdType.MESH
LANES = 128
WEIGHTS = (
    (1.0 / 3.0, (-1.0 / 36.0, -7.0 / 9.0, 0.0, 7.0 / 9.0, 1.0 / 36.0)),
    (2.0 / 11.0, (3.0 / 44.0, 12.0 / 11.0, -102.0 / 44.0, 12.0 / 11.0, 3.0 / 44.0)),
)


def constants():
    point = np.arange(LANES, dtype=np.float64)
    own, arrived = [], []
    leave = np.zeros((8, LANES))
    for which, (alpha, weights) in enumerate(WEIGHTS):
        ratio = (1.0 - np.sqrt(1.0 - 4.0 * alpha * alpha)) / (2.0 * alpha)
        factor = ratio / alpha / (1.0 - ratio * ratio)
        green = lambda d: factor * (-ratio) ** np.abs(d)
        kernel = lambda d: sum(w * green(d + k) for k, w in zip((-2, -1, 0, 1, 2), weights))
        own.append(kernel(point[None, :] - point[:, None]))
        rows = np.zeros((8, LANES))
        for side, sign in ((0, 1.0), (4, -1.0)):
            tail = kernel(sign * 2.0) / ratio**2
            away = point if side == 0 else LANES - 1 - point
            rows[side + which] = tail * (-ratio) ** (away + 1)
            rows[side + 2] = np.where(away == 0, kernel(sign) + tail * ratio, 0.0)
        arrived.append(rows)
        leave[which] = (-ratio) ** (LANES - 1 - point)
        leave[4 + which] = (-ratio) ** point
    leave[2, LANES - 1] = 1.0
    leave[6, 0] = 1.0
    return np.concatenate(own + arrived + [leave]).astype(np.float32)


def halves(array):
    high = array.astype(jnp.bfloat16)
    low = (array - high.astype(jnp.float32)).astype(jnp.bfloat16)
    return high, low


def kernel(
    places, groups, rows, points,
    x_hbm, const_hbm, index_hbm, jac_hbm, bend_hbm,
    first_hbm, second_hbm, energy_ref,
    x, const, index, jac_tab, bend_tab, split, first, second, op, edge_op,
    to_right, to_left, from_left, from_right, mine_a, slots_a, mine_b, slots_b,
    x_sem, in_sem, halo_send, halo_recv, a_send, a_recv, b_send, b_recv, out_sem,
):
    n_zh, n_y, n_core, n_zl, n_x = places
    n_gx = n_zh * n_y * n_core
    n_a, n_b = n_y * n_x, n_zh * n_zl * n_core
    gx, gz = lax.axis_index("gx"), lax.axis_index("gz")
    core = gx % n_core
    y = (gx // n_core) % n_y
    zh = gx // (n_core * n_y)
    xx = gz % n_x
    zl = gz // n_x
    in_a = y * n_x + xx
    in_b = (zh * n_zl + zl) * n_core + core

    def device_a(k):
        other = (in_a + k) % n_a
        return {"gx": (zh * n_y + other // n_x) * n_core + core, "gz": zl * n_x + other % n_x}

    def device_b(k):
        other = (in_b + k) % n_b
        other_z = other // n_core
        return {
            "gx": ((other_z // n_zl) * n_y + y) * n_core + other % n_core,
            "gz": (other_z % n_zl) * n_x + xx,
        }

    right = {"gx": (gx + 1) % n_gx, "gz": gz}
    left = {"gx": (gx + n_gx - 1) % n_gx, "gz": gz}

    def chunk(g):
        return pl.ds(pl.multiple_of(g * rows, rows), rows)

    def load(g):
        return pltpu.make_async_copy(x_hbm.at[chunk(g)], x.at[chunk(g)], x_sem.at[g])

    smalls = [
        pltpu.make_async_copy(src, dst, in_sem.at[n])
        for n, (src, dst) in enumerate(
            ((const_hbm, const), (index_hbm, index), (jac_hbm, jac_tab), (bend_hbm, bend_tab))
        )
    ]
    barrier = pltpu.get_barrier_semaphore()
    pl.semaphore_signal(barrier, inc=1, device_id=right, device_id_type=MESH)
    pl.semaphore_signal(barrier, inc=1, device_id=left, device_id_type=MESH)
    smalls[0].start()
    for g in range(groups):
        load(g).start()
    for copy in smalls[1:]:
        copy.start()

    @pl.loop(1, n_a)
    def _(k):
        pl.semaphore_signal(barrier, inc=1, device_id=device_a(k), device_id_type=MESH)

    @pl.loop(1, n_b)
    def _(k):
        pl.semaphore_signal(barrier, inc=1, device_id=device_b(k), device_id_type=MESH)

    smalls[0].wait()
    leave_high, leave_low = halves(const[272:280, :])
    leave = jnp.concatenate(
        [
            jnp.concatenate([leave_high, leave_high], axis=1),
            jnp.concatenate([leave_low, leave_low], axis=1),
        ],
        axis=0,
    )

    @pl.loop(0, groups)
    def _(g):
        load(g).wait()
        high, low = halves(x[chunk(g), :])
        both = jnp.concatenate([high, low], axis=1)
        split[chunk(g), :] = both
        sums = lax.dot_general(
            leave, both, (((1,), (1,)), ((), ())), preferred_element_type=jnp.float32
        )
        sums = sums[0:8] + sums[8:16]
        to_right[:, chunk(g)] = sums[0:4]
        to_left[:, chunk(g)] = sums[4:8]

    pl.semaphore_wait(barrier, 2 + (n_a - 1) + (n_b - 1))
    halo_r = pltpu.make_async_remote_copy(
        to_right, from_left, halo_send.at[0], halo_recv.at[0], device_id=right, device_id_type=MESH
    )
    halo_l = pltpu.make_async_remote_copy(
        to_left, from_right, halo_send.at[1], halo_recv.at[1], device_id=left, device_id_type=MESH
    )
    halo_r.start()
    halo_l.start()

    for copy in smalls[1:]:
        copy.wait()
    table_rows = jac_tab.shape[1]
    onehot = (
        lax.broadcasted_iota(jnp.int32, (table_rows, LANES), 0) == index[...]
    ).astype(jnp.float32)
    tables = jnp.concatenate(
        [jnp.broadcast_to(jac_tab[...], (8, table_rows)), jnp.broadcast_to(bend_tab[...], (8, table_rows))],
        axis=0,
    )
    metric = jnp.dot(tables, onehot, precision=lax.Precision.HIGHEST)
    inv_jac = 1.0 / metric[0:1]
    bend = metric[8:9]

    def scaled(one, two):
        one = one * inv_jac
        return jnp.concatenate([one, (two - bend * one) * (inv_jac * inv_jac)], axis=1)

    op_high, op_low = halves(scaled(const[0:128, :], const[128:256, :]))
    op[0:128, :] = op_high
    op[128:256, :] = op_low
    edge_high, edge_low = halves(scaled(const[256:264, :], const[264:272, :]))
    edge_op[...] = jnp.concatenate([edge_high, edge_high, edge_low, edge_low], axis=0)

    @pl.loop(0, groups)
    def _(g):
        both = split[chunk(g), :]
        high = op[0:128, :]
        low = op[128:256, :]
        part = jnp.dot(
            both, jnp.concatenate([high, high], axis=0), preferred_element_type=jnp.float32
        ) + jnp.dot(both, jnp.concatenate([low, low], axis=0), preferred_element_type=jnp.float32)
        first[chunk(g), :] = part[:, :LANES]
        second[chunk(g), :] = part[:, LANES:]

    halo_r.wait()
    halo_l.wait()
    lane = lax.broadcasted_iota(jnp.int32, (1, LANES), 1)

    def finish(g, energy):
        edge = jnp.concatenate([from_left[:, chunk(g)], from_right[:, chunk(g)]], axis=0)
        high = edge.astype(jnp.bfloat16).astype(jnp.float32)
        low = edge - high
        edge = jnp.concatenate([high, low, high, low], axis=0).T.astype(jnp.bfloat16)
        more = jnp.dot(edge, edge_op[...], preferred_element_type=jnp.float32)
        one = first[chunk(g), :] + more[:, :LANES]
        first[chunk(g), :] = one
        second[chunk(g), :] = second[chunk(g), :] + more[:, LANES:]
        square = jnp.sum(one * one, axis=0, keepdims=True)
        return energy + jnp.where(lane == g, jnp.sum(square, axis=1, keepdims=True), 0.0)

    energy = lax.fori_loop(0, groups, finish, jnp.zeros((1, LANES), jnp.float32))

    outs = [
        pltpu.make_async_copy(first, first_hbm, out_sem.at[0]),
        pltpu.make_async_copy(second, second_hbm, out_sem.at[1]),
    ]

    def send(n, here, mine, slots, device, send_sem, recv_sem):
        @pl.loop(1, n)
        def _(k):
            pltpu.make_async_remote_copy(
                mine, slots.at[here], send_sem, recv_sem, device_id=device(k), device_id_type=MESH
            ).start()

    def collect(n, slots, send_sem, recv_sem):
        rest = slots.at[pl.ds(0, n - 1)]
        pltpu.make_async_copy(rest, rest, recv_sem).wait()
        pltpu.make_async_copy(rest, rest, send_sem).wait()

    mine_a[...] = energy
    slots_a[in_a] = energy
    send(n_a, in_a, mine_a, slots_a, device_a, a_send, a_recv)
    for copy in outs:
        copy.start()
    collect(n_a, slots_a, a_send, a_recv)
    energy = jnp.sum(slots_a[...], axis=0)
    mine_b[...] = energy
    slots_b[in_b] = energy
    send(n_b, in_b, mine_b, slots_b, device_b, b_send, b_recv)
    collect(n_b, slots_b, b_send, b_recv)
    energy = jnp.sum(slots_b[...], axis=0) * (1.0 / points)
    width = energy_ref.shape[1]
    for row in range(energy_ref.shape[0]):
        energy_ref[row : row + 1, :] = energy[:, row * width : (row + 1) * width]
    for copy in outs:
        copy.wait()


def on_device(places, velocity, metric_index, jac_table, bend_table):
    n_zh, n_y, n_core, n_zl, n_x = places
    comps, planes, rows, lanes = velocity.shape
    groups = comps * planes
    lines = groups * rows
    table_rows = jac_table.shape[0]
    points = rows * n_zl * n_x * lanes * n_zh * n_y * n_core
    n_a, n_b = n_y * n_x, n_zh * n_zl * n_core
    f32, bf16 = jnp.float32, jnp.bfloat16
    const = jnp.asarray(constants())
    anywhere = pl.BlockSpec(memory_space=pl.ANY)
    dma = pltpu.SemaphoreType.DMA
    first, second, energy = pl.pallas_call(
        functools.partial(kernel, places, groups, rows, points),
        out_shape=(
            jax.ShapeDtypeStruct((lines, lanes), f32),
            jax.ShapeDtypeStruct((lines, lanes), f32),
            jax.ShapeDtypeStruct((comps, planes), f32),
        ),
        in_specs=[anywhere] * 5,
        out_specs=(anywhere, anywhere, pl.BlockSpec(memory_space=pltpu.VMEM)),
        scratch_shapes=[
            pltpu.VMEM((lines, lanes), f32),
            pltpu.VMEM(const.shape, f32),
            pltpu.VMEM((1, lanes), jnp.int32),
            pltpu.VMEM((1, table_rows), f32),
            pltpu.VMEM((1, table_rows), f32),
            pltpu.VMEM((lines, 2 * lanes), bf16),
            pltpu.VMEM((lines, lanes), f32),
            pltpu.VMEM((lines, lanes), f32),
            pltpu.VMEM((2 * lanes, 2 * lanes), bf16),
            pltpu.VMEM((32, 2 * lanes), bf16),
            pltpu.VMEM((4, lines), f32),
            pltpu.VMEM((4, lines), f32),
            pltpu.VMEM((4, lines), f32),
            pltpu.VMEM((4, lines), f32),
            pltpu.VMEM((1, lanes), f32),
            pltpu.VMEM((n_a, 1, lanes), f32),
            pltpu.VMEM((1, lanes), f32),
            pltpu.VMEM((n_b, 1, lanes), f32),
            dma((groups,)),
            dma((4,)),
            dma((2,)),
            dma((2,)),
            dma, dma, dma, dma,
            dma((2,)),
        ],
        compiler_params=pltpu.CompilerParams(collective_id=0, has_side_effects=True),
    )(
        velocity.reshape(lines, lanes),
        const,
        metric_index.reshape(1, lanes),
        jac_table.reshape(1, table_rows),
        bend_table.reshape(1, table_rows),
    )
    return (first.reshape(velocity.shape), second.reshape(velocity.shape), energy)


def solution(mesh):
    n_gx, n_gz = mesh.shape["gx"], mesh.shape["gz"]
    n_x = min(4, n_gz)
    places = (2, n_gx // 4, 2, n_gz // n_x, n_x)
    in_specs = (P(None, None, "gz", "gx"), P("gx"), P(), P())
    out_specs = (P(None, None, "gz", "gx"), P(None, None, "gz", "gx"), P())
    return jax.shard_map(
        functools.partial(on_device, places),
        mesh=mesh, in_specs=in_specs, out_specs=out_specs, check_vma=False,
    )
```

```python
import functools

import jax
import jax.numpy as jnp
import numpy as np
from jax import lax
from jax.experimental import pallas as pl
from jax.experimental.pallas import tpu as pltpu
from jax.sharding import PartitionSpec as P


MESH = pl.DeviceIdType.MESH
LANES = 128
WEIGHTS = (
    (1.0 / 3.0, (-1.0 / 36.0, -7.0 / 9.0, 0.0, 7.0 / 9.0, 1.0 / 36.0)),
    (2.0 / 11.0, (3.0 / 44.0, 12.0 / 11.0, -102.0 / 44.0, 12.0 / 11.0, 3.0 / 44.0)),
)


def constants():
    point = np.arange(LANES, dtype=np.float64)
    own, arrived = [], []
    leave = np.zeros((8, LANES))
    for which, (alpha, weights) in enumerate(WEIGHTS):
        ratio = (1.0 - np.sqrt(1.0 - 4.0 * alpha * alpha)) / (2.0 * alpha)
        factor = ratio / alpha / (1.0 - ratio * ratio)
        green = lambda d: factor * (-ratio) ** np.abs(d)
        kernel = lambda d: sum(w * green(d + k) for k, w in zip((-2, -1, 0, 1, 2), weights))
        own.append(kernel(point[None, :] - point[:, None]))
        rows = np.zeros((8, LANES))
        for side, sign in ((0, 1.0), (4, -1.0)):
            tail = kernel(sign * 2.0) / ratio**2
            away = point if side == 0 else LANES - 1 - point
            rows[side + which] = tail * (-ratio) ** (away + 1)
            rows[side + 2] = np.where(away == 0, kernel(sign) + tail * ratio, 0.0)
        arrived.append(rows)
        leave[which] = (-ratio) ** (LANES - 1 - point)
        leave[4 + which] = (-ratio) ** point
    leave[2, LANES - 1] = 1.0
    leave[6, 0] = 1.0
    return np.concatenate(own + arrived + [leave]).astype(np.float32)


def halves(array):
    high = array.astype(jnp.bfloat16)
    low = (array - high.astype(jnp.float32)).astype(jnp.bfloat16)
    return high, low


def kernel(
    places, groups, rows, points,
    x_hbm, const_hbm, index_hbm, jac_hbm, bend_hbm,
    first, second, energy_ref,
    x, const, index, jac_tab, bend_tab, split, edge_t, op, edge_op, squares,
    to_right, to_left, from_left, from_right, mine_a, slots_a, mine_b, slots_b,
    x_sem, in_sem, halo_send, halo_recv, a_send, a_recv, b_send, b_recv,
):
    n_zh, n_y, n_core, n_zl, n_x = places
    n_gx = n_zh * n_y * n_core
    n_z = n_zh * n_zl
    halves_x = n_x // 2
    n_a, n_b = n_y * 2, n_z * n_core * halves_x
    gx, gz = lax.axis_index("gx"), lax.axis_index("gz")
    core = gx % n_core
    y = (gx // n_core) % n_y
    zh = gx // (n_core * n_y)
    xx = gz % n_x
    zl = gz // n_x
    z = zh * n_zl + zl
    in_a = y * 2 + xx % 2
    in_b = (z * n_core + core) * halves_x + xx // 2

    def turned(place, by, size):
        place = place + by
        return jnp.where(place >= size, place - size, place)

    pair_a = xx + 1 - 2 * (xx % 2)
    ys = [(zh * n_y + turned(y, by, n_y)) * n_core + core for by in range(n_y)]
    peers_a = [
        (min(by, n_y - by) + across, ys[by], zl * n_x + (pair_a if across else xx))
        for by in range(n_y) for across in range(2) if by + across
    ]
    zs = [turned(z, by, n_z) for by in range(n_z)]
    peers_b = [
        (
            min(by, n_z - by) + across,
            ((zs[by] // n_zl) * n_y + y) * n_core + (1 - core if other else core),
            (zs[by] % n_zl) * n_x + (n_x - 1 - xx if across else xx),
        )
        for by in range(n_z) for other in range(n_core) for across in range(halves_x) if by + other + across
    ]
    peers_a = [{"gx": p[1], "gz": p[2]} for p in sorted(peers_a, key=lambda p: -p[0])]
    peers_b = [{"gx": p[1], "gz": p[2]} for p in sorted(peers_b, key=lambda p: -p[0])]

    right = {"gx": (gx + 1) % n_gx, "gz": gz}
    left = {"gx": (gx + n_gx - 1) % n_gx, "gz": gz}

    def chunk(g):
        return pl.ds(pl.multiple_of(g * rows, rows), rows)

    def load(g):
        return pltpu.make_async_copy(x_hbm.at[chunk(g)], x.at[chunk(g)], x_sem.at[g])

    smalls = [
        pltpu.make_async_copy(src, dst, in_sem.at[n])
        for n, (src, dst) in enumerate(
            ((const_hbm, const), (index_hbm, index), (jac_hbm, jac_tab), (bend_hbm, bend_tab))
        )
    ]
    barrier = pltpu.get_barrier_semaphore()
    pl.semaphore_signal(barrier, inc=1, device_id=right, device_id_type=MESH)
    pl.semaphore_signal(barrier, inc=1, device_id=left, device_id_type=MESH)
    smalls[0].start()
    for g in range(groups):
        load(g).start()
    for copy in smalls[1:]:
        copy.start()

    for peer in peers_a + peers_b:
        pl.semaphore_signal(barrier, inc=1, device_id=peer, device_id_type=MESH)

    smalls[0].wait()
    leave_high, leave_low = halves(const[272:280, :])
    leave = jnp.concatenate(
        [
            jnp.concatenate([leave_high, leave_high], axis=1),
            jnp.concatenate([leave_low, leave_low], axis=1),
        ],
        axis=0,
    )

    @pl.loop(0, groups)
    def _(g):
        load(g).wait()
        high, low = halves(x[chunk(g), :])
        both = jnp.concatenate([high, low], axis=1)
        split[chunk(g), :] = both
        sums = lax.dot_general(
            leave, both, (((1,), (1,)), ((), ())), preferred_element_type=jnp.float32
        )
        sums = sums[0:8] + sums[8:16]
        to_right[:, chunk(g)] = sums[0:4]
        to_left[:, chunk(g)] = sums[4:8]

    pl.semaphore_wait(barrier, 2 + (n_a - 1) + (n_b - 1))
    halo_r = pltpu.make_async_remote_copy(
        to_right, from_left, halo_send.at[0], halo_recv.at[0], device_id=right, device_id_type=MESH
    )
    halo_l = pltpu.make_async_remote_copy(
        to_left, from_right, halo_send.at[1], halo_recv.at[1], device_id=left, device_id_type=MESH
    )
    halo_r.start()
    halo_l.start()

    for copy in smalls[1:]:
        copy.wait()
    table_rows = jac_tab.shape[1]
    onehot = (
        lax.broadcasted_iota(jnp.int32, (table_rows, LANES), 0) == index[...]
    ).astype(jnp.float32)
    tables = jnp.concatenate(
        [jnp.broadcast_to(jac_tab[...], (8, table_rows)), jnp.broadcast_to(bend_tab[...], (8, table_rows))],
        axis=0,
    )
    metric = jnp.dot(tables, onehot, precision=lax.Precision.HIGHEST)
    inv_jac = 1.0 / metric[0:1]
    bend = metric[8:9]

    def scaled(one, two):
        one = one * inv_jac
        return jnp.concatenate([one, (two - bend * one) * (inv_jac * inv_jac)], axis=1)

    op_high, op_low = halves(scaled(const[0:128, :], const[128:256, :]))
    op[0:128, :] = op_high
    op[128:256, :] = op_low
    edge_high, edge_low = halves(scaled(const[256:264, :], const[264:272, :]))
    edge_op[...] = jnp.concatenate([edge_high, edge_high, edge_low, edge_low], axis=0)

    @pl.loop(0, groups)
    def _(g):
        both = split[chunk(g), :]
        high = op[0:128, :]
        low = op[128:256, :]
        part = jnp.dot(
            both, jnp.concatenate([high, high], axis=0), preferred_element_type=jnp.float32
        ) + jnp.dot(both, jnp.concatenate([low, low], axis=0), preferred_element_type=jnp.float32)
        first[chunk(g), :] = part[:, :LANES]
        second[chunk(g), :] = part[:, LANES:]

    halo_r.wait()
    halo_l.wait()

    squares[...] = jnp.zeros_like(squares)

    @pl.loop(0, groups)
    def _(g):
        edge = jnp.concatenate([from_left[:, chunk(g)], from_right[:, chunk(g)]], axis=0)
        high = edge.astype(jnp.bfloat16).astype(jnp.float32)
        low = edge - high
        edge = jnp.concatenate([high, low, high, low], axis=0).T.astype(jnp.bfloat16)
        edge_t[chunk(g), :] = edge
        more = jnp.dot(edge, edge_op[:, :LANES], preferred_element_type=jnp.float32)
        one = first[chunk(g), :] + more
        first[chunk(g), :] = one
        squares[pl.ds(g, 1), :] = jnp.sum(one * one, axis=0, keepdims=True)

    def send(here, mine, slots, peers, send_sem, recv_sem):
        for peer in peers:
            pltpu.make_async_remote_copy(
                mine, slots.at[here], send_sem, recv_sem, device_id=peer, device_id_type=MESH
            ).start()

    def collect(n, slots, send_sem, recv_sem):
        rest = slots.at[pl.ds(0, n - 1)]
        pltpu.make_async_copy(rest, rest, recv_sem).wait()
        pltpu.make_async_copy(rest, rest, send_sem).wait()

    diagonal = lax.broadcasted_iota(jnp.int32, (8, LANES), 0) == lax.broadcasted_iota(
        jnp.int32, (8, LANES), 1
    )
    energy = jnp.sum(squares[...], axis=1, keepdims=True)
    energy = jnp.sum(jnp.where(diagonal, energy, 0.0), axis=0, keepdims=True)
    mine_a[...] = energy
    slots_a[in_a] = energy
    send(in_a, mine_a, slots_a, peers_a, a_send, a_recv)

    @pl.loop(0, groups)
    def _(g):
        more = jnp.dot(edge_t[chunk(g), :], edge_op[:, LANES:], preferred_element_type=jnp.float32)
        second[chunk(g), :] = second[chunk(g), :] + more

    collect(n_a, slots_a, a_send, a_recv)
    energy = jnp.sum(slots_a[...], axis=0)
    mine_b[...] = energy
    slots_b[in_b] = energy
    send(in_b, mine_b, slots_b, peers_b, b_send, b_recv)
    collect(n_b, slots_b, b_send, b_recv)
    energy_ref[...] = jnp.sum(slots_b[...], axis=0) * (1.0 / points)


def store(first, second, energy_ref, first_hbm, second_hbm, out_ref, sems):
    outs = [
        pltpu.make_async_copy(first, first_hbm, sems.at[0]),
        pltpu.make_async_copy(second, second_hbm, sems.at[1]),
    ]
    for copy in outs:
        copy.start()
    planes, comps = out_ref.shape
    energy = energy_ref[...]
    for row in range(planes):
        for col in range(comps):
            at = col * planes + row
            out_ref[row : row + 1, col : col + 1] = energy[:, at : at + 1]
    for copy in outs:
        copy.wait()


def on_device(places, velocity, metric_index, jac_table, bend_table):
    n_zh, n_y, n_core, n_zl, n_x = places
    comps, planes, rows, lanes = velocity.shape
    groups = comps * planes
    lines = groups * rows
    table_rows = jac_table.shape[0]
    points = rows * n_zl * n_x * lanes * n_zh * n_y * n_core
    n_a, n_b = n_y * 2, n_zh * n_zl * n_core * (n_x // 2)
    f32, bf16 = jnp.float32, jnp.bfloat16
    const = jnp.asarray(constants())
    anywhere = pl.BlockSpec(memory_space=pl.ANY)
    vmem = pl.BlockSpec(memory_space=pltpu.VMEM)
    dma = pltpu.SemaphoreType.DMA
    first, second, energy = pl.pallas_call(
        functools.partial(kernel, places, groups, rows, points),
        out_shape=(
            pltpu.VMEM((lines, lanes), f32),
            pltpu.VMEM((lines, lanes), f32),
            pltpu.VMEM((1, lanes), f32),
        ),
        in_specs=[anywhere] * 5,
        out_specs=(vmem, vmem, vmem),
        scratch_shapes=[
            pltpu.VMEM((lines, lanes), f32),
            pltpu.VMEM(const.shape, f32),
            pltpu.VMEM((1, lanes), jnp.int32),
            pltpu.VMEM((1, table_rows), f32),
            pltpu.VMEM((1, table_rows), f32),
            pltpu.VMEM((lines, 2 * lanes), bf16),
            pltpu.VMEM((lines, 32), bf16),
            pltpu.VMEM((2 * lanes, 2 * lanes), bf16),
            pltpu.VMEM((32, 2 * lanes), bf16),
            pltpu.VMEM((8, lanes), f32),
            pltpu.VMEM((4, lines), f32),
            pltpu.VMEM((4, lines), f32),
            pltpu.VMEM((4, lines), f32),
            pltpu.VMEM((4, lines), f32),
            pltpu.VMEM((1, lanes), f32),
            pltpu.VMEM((n_a, 1, lanes), f32),
            pltpu.VMEM((1, lanes), f32),
            pltpu.VMEM((n_b, 1, lanes), f32),
            dma((groups,)),
            dma((4,)),
            dma((2,)),
            dma((2,)),
            dma, dma, dma, dma,
        ],
        compiler_params=pltpu.CompilerParams(collective_id=0, has_side_effects=True),
    )(
        velocity.reshape(lines, lanes),
        const,
        metric_index.reshape(1, lanes),
        jac_table.reshape(1, table_rows),
        bend_table.reshape(1, table_rows),
    )
    whole = jax.ShapeDtypeStruct((lines, lanes), f32)
    first, second, energy = pl.pallas_call(
        store,
        out_shape=(whole, whole, jax.ShapeDtypeStruct((planes, comps), f32)),
        in_specs=[vmem] * 3,
        out_specs=(anywhere, anywhere, vmem),
        scratch_shapes=[dma((2,))],
    )(*(pltpu.with_memory_space_constraint(a, pltpu.VMEM) for a in (first, second, energy)))
    return (first.reshape(velocity.shape), second.reshape(velocity.shape), energy.T)


def solution(mesh):
    n_gx, n_gz = mesh.shape["gx"], mesh.shape["gz"]
    n_x = min(4, n_gz)
    places = (2, n_gx // 4, 2, n_gz // n_x, n_x)
    in_specs = (P(None, None, "gz", "gx"), P("gx"), P(), P())
    out_specs = (P(None, None, "gz", "gx"), P(None, None, "gz", "gx"), P())
    return jax.shard_map(
        functools.partial(on_device, places),
        mesh=mesh, in_specs=in_specs, out_specs=out_specs, check_vma=False,
    )
```

```python
import functools

import jax
import jax.numpy as jnp
import numpy as np
from jax import lax
from jax.experimental import pallas as pl
from jax.experimental.pallas import tpu as pltpu
from jax.sharding import PartitionSpec as P


MESH = pl.DeviceIdType.MESH
LANES = 128
WEIGHTS = (
    (1.0 / 3.0, (-1.0 / 36.0, -7.0 / 9.0, 0.0, 7.0 / 9.0, 1.0 / 36.0)),
    (2.0 / 11.0, (3.0 / 44.0, 12.0 / 11.0, -102.0 / 44.0, 12.0 / 11.0, 3.0 / 44.0)),
)


def constants():
    point = np.arange(LANES, dtype=np.float64)
    own, arrived = [], []
    leave = np.zeros((8, LANES))
    for which, (alpha, weights) in enumerate(WEIGHTS):
        ratio = (1.0 - np.sqrt(1.0 - 4.0 * alpha * alpha)) / (2.0 * alpha)
        factor = ratio / alpha / (1.0 - ratio * ratio)
        green = lambda d: factor * (-ratio) ** np.abs(d)
        kernel = lambda d: sum(w * green(d + k) for k, w in zip((-2, -1, 0, 1, 2), weights))
        own.append(kernel(point[None, :] - point[:, None]))
        rows = np.zeros((8, LANES))
        for side, sign in ((0, 1.0), (4, -1.0)):
            tail = kernel(sign * 2.0) / ratio**2
            away = point if side == 0 else LANES - 1 - point
            rows[side + which] = tail * (-ratio) ** (away + 1)
            rows[side + 2] = np.where(away == 0, kernel(sign) + tail * ratio, 0.0)
        arrived.append(rows)
        leave[which] = (-ratio) ** (LANES - 1 - point)
        leave[4 + which] = (-ratio) ** point
    leave[2, LANES - 1] = 1.0
    leave[6, 0] = 1.0
    return np.concatenate(own + arrived + [leave]).astype(np.float32)


def halves(array):
    high = array.astype(jnp.bfloat16)
    low = (array - high.astype(jnp.float32)).astype(jnp.bfloat16)
    return high, low


def kernel(
    places, groups, rows, points,
    x_hbm, const_hbm, index_hbm, jac_hbm, bend_hbm,
    first, second, energy_ref,
    x, const, index, jac_tab, bend_tab, split, edge_t, op, edge_op, squares,
    to_right, to_left, from_left, from_right, from_far, to_middle_r, to_middle_l, middle,
    mine_a, slots_a, mine_b, slots_b,
    x_sem, in_sem, halo_send, halo_recv, far_recv, mid_send, mid_recv, a_send, a_recv, b_send, b_recv,
):
    n_zh, n_y, n_core, n_zl, n_x = places
    n_gx = n_zh * n_y * n_core
    n_z = n_zh * n_zl
    halves_x = n_x // 2
    n_a, n_b = n_y * 2, n_z * n_core * halves_x
    gx, gz = lax.axis_index("gx"), lax.axis_index("gz")
    core = gx % n_core
    y = (gx // n_core) % n_y
    zh = gx // (n_core * n_y)
    xx = gz % n_x
    zl = gz // n_x
    z = zh * n_zl + zl
    in_a = y * 2 + xx % 2
    in_b = (z * n_core + core) * halves_x + xx // 2

    def turned(place, by, size):
        place = place + by
        return jnp.where(place >= size, place - size, place)

    pair_a = xx + 1 - 2 * (xx % 2)
    ys = [(zh * n_y + turned(y, by, n_y)) * n_core + core for by in range(n_y)]
    peers_a = [
        (min(by, n_y - by) + across, ys[by], zl * n_x + (pair_a if across else xx))
        for by in range(n_y) for across in range(2) if by + across
    ]
    zs = [turned(z, by, n_z) for by in range(n_z)]
    peers_b = [
        (
            min(by, n_z - by) + across,
            ((zs[by] // n_zl) * n_y + y) * n_core + (1 - core if other else core),
            (zs[by] % n_zl) * n_x + (n_x - 1 - xx if across else xx),
        )
        for by in range(n_z) for other in range(n_core) for across in range(halves_x) if by + other + across
    ]
    peers_a = [{"gx": p[1], "gz": p[2]} for p in sorted(peers_a, key=lambda p: -p[0])]
    peers_b = [{"gx": p[1], "gz": p[2]} for p in sorted(peers_b, key=lambda p: -p[0])]

    lines = groups * rows
    quarter = n_z // 4
    is_last = jnp.logical_and(y == n_y - 1, core == n_core - 1)
    is_first = jnp.logical_and(y == 0, core == 0)

    def in_z(by, at_last):
        there = turned(z, by % n_z, n_z)
        within = n_y * n_core - 1 if at_last else 0
        return {"gx": (there // n_zl) * n_y * n_core + within, "gz": (there % n_zl) * n_x + xx}

    ahead, behind = in_z(quarter, True), in_z(-quarter, True)
    ahead_first = in_z(quarter, False)

    right = {"gx": (gx + 1) % n_gx, "gz": gz}
    left = {"gx": (gx + n_gx - 1) % n_gx, "gz": gz}

    def chunk(g):
        return pl.ds(pl.multiple_of(g * rows, rows), rows)

    def load(g):
        return pltpu.make_async_copy(x_hbm.at[chunk(g)], x.at[chunk(g)], x_sem.at[g])

    smalls = [
        pltpu.make_async_copy(src, dst, in_sem.at[n])
        for n, (src, dst) in enumerate(
            ((const_hbm, const), (index_hbm, index), (jac_hbm, jac_tab), (bend_hbm, bend_tab))
        )
    ]
    barrier = pltpu.get_barrier_semaphore()
    pl.semaphore_signal(barrier, inc=1, device_id=right, device_id_type=MESH)
    pl.semaphore_signal(barrier, inc=1, device_id=left, device_id_type=MESH)
    for copy in smalls:
        copy.start()
    for g in range(groups):
        load(g).start()

    for peer in peers_a + peers_b:
        pl.semaphore_signal(barrier, inc=1, device_id=peer, device_id_type=MESH)

    @pl.when(is_last)
    def _():
        for peer in (ahead, behind, ahead_first):
            pl.semaphore_signal(barrier, inc=1, device_id=peer, device_id_type=MESH)
        from_right[...] = jnp.zeros_like(from_right)

    @pl.when(is_first)
    def _():
        pl.semaphore_signal(barrier, inc=1, device_id=behind, device_id_type=MESH)
        from_left[...] = jnp.zeros_like(from_left)

    for copy in smalls:
        copy.wait()
    table_rows = jac_tab.shape[1]
    onehot = (
        lax.broadcasted_iota(jnp.int32, (table_rows, LANES), 0) == index[...]
    ).astype(jnp.float32)
    tables = jnp.concatenate(
        [jnp.broadcast_to(jac_tab[...], (8, table_rows)), jnp.broadcast_to(bend_tab[...], (8, table_rows))],
        axis=0,
    )
    metric = jnp.dot(tables, onehot, precision=lax.Precision.HIGHEST)
    inv_jac = 1.0 / metric[0:1]
    bend = metric[8:9]

    def scaled(one, two):
        one = one * inv_jac
        return jnp.concatenate([one, (two - bend * one) * (inv_jac * inv_jac)], axis=1)

    own_op = scaled(const[0:128, :], const[128:256, :])
    arrived_op = scaled(const[256:264, :], const[264:272, :])
    arrived_one = arrived_op[:, :LANES]
    joint = lax.dot_general(
        arrived_one, own_op[:, :LANES], (((1,), (1,)), ((), ())),
        precision=lax.Precision.HIGHEST, preferred_element_type=jnp.float32,
    )
    for ref, at in ((to_middle_l, 0), (to_middle_r, 4)):
        sums_of, edge_of = arrived_one[at : at + 1], arrived_one[at + 2 : at + 3]
        for row, (product, times) in enumerate(
            ((sums_of * sums_of, 1.0), (sums_of * edge_of, 2.0), (edge_of * edge_of, 1.0))
        ):
            total = jnp.sum(product, axis=1, keepdims=True) * times
            ref[row : row + 1, lines:] = jnp.broadcast_to(total, (1, LANES))
        ref[3:4, lines:] = jnp.zeros((1, LANES), jnp.float32)
    out_rows = const[272:280, :]
    leave_high, leave_low = halves(
        jnp.concatenate(
            [
                out_rows,
                out_rows[0:1], out_rows[2:3], joint[4:5], joint[6:7],
                out_rows[4:5], out_rows[6:7], joint[0:1], joint[2:3],
            ],
            axis=0,
        )
    )
    leave = jnp.concatenate(
        [
            jnp.concatenate([leave_high, leave_high], axis=1),
            jnp.concatenate([leave_low, leave_low], axis=1),
        ],
        axis=0,
    )

    @pl.loop(0, groups)
    def _(g):
        load(g).wait()
        high, low = halves(x[chunk(g), :])
        both = jnp.concatenate([high, low], axis=1)
        split[chunk(g), :] = both
        sums = lax.dot_general(
            leave, both, (((1,), (1,)), ((), ())), preferred_element_type=jnp.float32
        )
        sums = sums[0:16] + sums[16:32]
        to_right[:, chunk(g)] = sums[0:4]
        to_left[:, chunk(g)] = sums[4:8]
        to_middle_r[:, chunk(g)] = sums[8:12]
        to_middle_l[:, chunk(g)] = sums[12:16]

    pl.semaphore_wait(
        barrier, 2 + (n_a - 1) + (n_b - 1) + jnp.where(is_last, 3, jnp.where(is_first, 1, 0))
    )
    middle_r = pltpu.make_async_remote_copy(
        to_middle_r, middle.at[0], mid_send, mid_recv.at[0], device_id=ahead, device_id_type=MESH
    )
    middle_l = pltpu.make_async_remote_copy(
        to_middle_l, middle.at[1], mid_send, mid_recv.at[1], device_id=behind, device_id_type=MESH
    )
    halo_r = pltpu.make_async_remote_copy(
        to_right, from_left, halo_send.at[0], halo_recv.at[0], device_id=right, device_id_type=MESH
    )
    halo_l = pltpu.make_async_remote_copy(
        to_left, from_right, halo_send.at[1], halo_recv.at[1], device_id=left, device_id_type=MESH
    )
    far_r = pltpu.make_async_remote_copy(
        to_right, from_far, halo_send.at[0], far_recv, device_id=right, device_id_type=MESH
    )
    far_l = pltpu.make_async_remote_copy(
        to_left, from_far, halo_send.at[1], far_recv, device_id=left, device_id_type=MESH
    )

    @pl.when(is_last)
    def _():
        middle_r.start()
        halo_l.start()
        far_r.start()

    @pl.when(is_first)
    def _():
        middle_l.start()
        halo_r.start()
        far_l.start()

    is_inner = jnp.logical_not(jnp.logical_or(is_last, is_first))

    @pl.when(is_inner)
    def _():
        halo_r.start()
        halo_l.start()

    op_high, op_low = halves(own_op)
    op[0:128, :] = op_high
    op[128:256, :] = op_low
    edge_high, edge_low = halves(arrived_op)
    edge_op[...] = jnp.concatenate([edge_high, edge_high, edge_low, edge_low], axis=0)

    @pl.loop(0, groups)
    def _(g):
        both = split[chunk(g), :]
        high = op[0:128, :]
        low = op[128:256, :]
        part = jnp.dot(
            both, jnp.concatenate([high, high], axis=0), preferred_element_type=jnp.float32
        ) + jnp.dot(both, jnp.concatenate([low, low], axis=0), preferred_element_type=jnp.float32)
        first[chunk(g), :] = part[:, :LANES]
        second[chunk(g), :] = part[:, LANES:]

    @pl.when(jnp.logical_not(is_first))
    def _():
        halo_r.wait_recv()

    @pl.when(jnp.logical_not(is_last))
    def _():
        halo_l.wait_recv()

    def spread(left_edge, right_edge):
        edge = jnp.concatenate([left_edge, right_edge], axis=0)
        high = edge.astype(jnp.bfloat16).astype(jnp.float32)
        low = edge - high
        return jnp.concatenate([high, low, high, low], axis=0).T.astype(jnp.bfloat16)

    squares[...] = jnp.zeros_like(squares)

    @pl.loop(0, groups)
    def _(g):
        edge = spread(from_left[:, chunk(g)], from_right[:, chunk(g)])
        edge_t[chunk(g), :] = edge
        more = jnp.dot(edge, edge_op[:, :LANES], preferred_element_type=jnp.float32)
        one = first[chunk(g), :] + more
        first[chunk(g), :] = one
        squares[pl.ds(g, 1), :] = jnp.sum(one * one, axis=0, keepdims=True)

    @pl.when(is_last)
    def _():
        middle_r.wait_recv()
        middle_l.wait_recv()
        whole = pl.ds(0, lines)
        right_sum, right_edge = middle[0, 0:1, whole], middle[0, 1:2, whole]
        left_sum, left_edge = middle[1, 0:1, whole], middle[1, 1:2, whole]

        def again(side, row):
            return jnp.concatenate([middle[side, row : row + 1, lines:]] * (lines // LANES), axis=1)

        cross = 2.0 * (
            right_sum * middle[1, 2:3, whole] + right_edge * middle[1, 3:4, whole]
            + left_sum * middle[0, 2:3, whole] + left_edge * middle[0, 3:4, whole]
        )
        for side, some, edge in ((1, right_sum, right_edge), (0, left_sum, left_edge)):
            cross += some * (again(side, 0) * some + again(side, 1) * edge) + again(side, 2) * edge * edge
        for g in range(groups):
            total = squares[g : g + 1, :]
            for at in range(g * rows, (g + 1) * rows, LANES):
                total += cross[:, at : at + LANES]
            squares[g : g + 1, :] = total

    def send(here, mine, slots, peers, send_sem, recv_sem):
        for peer in peers:
            pltpu.make_async_remote_copy(
                mine, slots.at[here], send_sem, recv_sem, device_id=peer, device_id_type=MESH
            ).start()

    def collect(n, slots, send_sem, recv_sem):
        rest = slots.at[pl.ds(0, n - 1)]
        pltpu.make_async_copy(rest, rest, recv_sem).wait()
        pltpu.make_async_copy(rest, rest, send_sem).wait()

    diagonal = lax.broadcasted_iota(jnp.int32, (8, LANES), 0) == lax.broadcasted_iota(
        jnp.int32, (8, LANES), 1
    )
    energy = jnp.sum(squares[...], axis=1, keepdims=True)
    energy = jnp.sum(jnp.where(diagonal, energy, 0.0), axis=0, keepdims=True)
    mine_a[...] = energy
    slots_a[in_a] = energy
    send(in_a, mine_a, slots_a, peers_a, a_send, a_recv)

    @pl.loop(0, groups)
    def _(g):
        more = jnp.dot(edge_t[chunk(g), :], edge_op[:, LANES:], preferred_element_type=jnp.float32)
        second[chunk(g), :] = second[chunk(g), :] + more

    @pl.when(jnp.logical_not(is_inner))
    def _():
        far_r.wait_recv()

        @pl.loop(0, groups)
        def _(g):
            far = from_far[:, chunk(g)]
            edge = spread(jnp.where(is_first, far, 0.0), jnp.where(is_last, far, 0.0))
            more = jnp.dot(edge, edge_op[...], preferred_element_type=jnp.float32)
            first[chunk(g), :] = first[chunk(g), :] + more[:, :LANES]
            second[chunk(g), :] = second[chunk(g), :] + more[:, LANES:]

    collect(n_a, slots_a, a_send, a_recv)
    energy = jnp.sum(slots_a[...], axis=0)
    mine_b[...] = energy
    slots_b[in_b] = energy
    send(in_b, mine_b, slots_b, peers_b, b_send, b_recv)
    collect(n_b, slots_b, b_send, b_recv)
    energy_ref[...] = jnp.sum(slots_b[...], axis=0) * (1.0 / points)
    halo_r.wait_send()
    halo_l.wait_send()

    @pl.when(jnp.logical_not(is_inner))
    def _():
        middle_r.wait_send()


def store(first, second, energy_ref, first_hbm, second_hbm, out_ref, sems):
    lines, pieces = first.shape[0], sems.shape[1]
    step = lines // pieces
    outs = [
        pltpu.make_async_copy(src.at[pl.ds(n * step, step)], dst.at[pl.ds(n * step, step)], sems.at[side, n])
        for n in range(pieces)
        for side, (src, dst) in enumerate(((first, first_hbm), (second, second_hbm)))
    ]
    for copy in outs:
        copy.start()
    planes, comps = out_ref.shape
    energy = energy_ref[...]
    for row in range(planes):
        for col in range(comps):
            at = col * planes + row
            out_ref[row : row + 1, col : col + 1] = energy[:, at : at + 1]
    for copy in outs:
        copy.wait()


def on_device(places, velocity, metric_index, jac_table, bend_table):
    n_zh, n_y, n_core, n_zl, n_x = places
    comps, planes, rows, lanes = velocity.shape
    groups = comps * planes
    lines = groups * rows
    table_rows = jac_table.shape[0]
    points = rows * n_zl * n_x * lanes * n_zh * n_y * n_core
    n_a, n_b = n_y * 2, n_zh * n_zl * n_core * (n_x // 2)
    f32, bf16 = jnp.float32, jnp.bfloat16
    const = jnp.asarray(constants())
    anywhere = pl.BlockSpec(memory_space=pl.ANY)
    vmem = pl.BlockSpec(memory_space=pltpu.VMEM)
    dma = pltpu.SemaphoreType.DMA
    first, second, energy = pl.pallas_call(
        functools.partial(kernel, places, groups, rows, points),
        out_shape=(
            pltpu.VMEM((lines, lanes), f32),
            pltpu.VMEM((lines, lanes), f32),
            pltpu.VMEM((1, lanes), f32),
        ),
        in_specs=[anywhere] * 5,
        out_specs=(vmem, vmem, vmem),
        scratch_shapes=[
            pltpu.VMEM((lines, lanes), f32),
            pltpu.VMEM(const.shape, f32),
            pltpu.VMEM((1, lanes), jnp.int32),
            pltpu.VMEM((1, table_rows), f32),
            pltpu.VMEM((1, table_rows), f32),
            pltpu.VMEM((lines, 2 * lanes), bf16),
            pltpu.VMEM((lines, 32), bf16),
            pltpu.VMEM((2 * lanes, 2 * lanes), bf16),
            pltpu.VMEM((32, 2 * lanes), bf16),
            pltpu.VMEM((8, lanes), f32),
            pltpu.VMEM((4, lines), f32),
            pltpu.VMEM((4, lines), f32),
            pltpu.VMEM((4, lines), f32),
            pltpu.VMEM((4, lines), f32),
            pltpu.VMEM((4, lines), f32),
            pltpu.VMEM((4, lines + lanes), f32),
            pltpu.VMEM((4, lines + lanes), f32),
            pltpu.VMEM((2, 4, lines + lanes), f32),
            pltpu.VMEM((1, lanes), f32),
            pltpu.VMEM((n_a, 1, lanes), f32),
            pltpu.VMEM((1, lanes), f32),
            pltpu.VMEM((n_b, 1, lanes), f32),
            dma((groups,)),
            dma((4,)),
            dma((2,)),
            dma((2,)),
            dma,
            dma,
            dma((2,)),
            dma, dma, dma, dma,
        ],
        compiler_params=pltpu.CompilerParams(collective_id=0, has_side_effects=True),
    )(
        velocity.reshape(lines, lanes),
        const,
        metric_index.reshape(1, lanes),
        jac_table.reshape(1, table_rows),
        bend_table.reshape(1, table_rows),
    )
    whole = jax.ShapeDtypeStruct((lines, lanes), f32)
    first, second, energy = pl.pallas_call(
        store,
        out_shape=(whole, whole, jax.ShapeDtypeStruct((planes, comps), f32)),
        in_specs=[vmem] * 3,
        out_specs=(anywhere, anywhere, vmem),
        scratch_shapes=[dma((2, groups))],
    )(*(pltpu.with_memory_space_constraint(a, pltpu.VMEM) for a in (first, second, energy)))
    return (first.reshape(velocity.shape), second.reshape(velocity.shape), energy.T)


def solution(mesh):
    n_gx, n_gz = mesh.shape["gx"], mesh.shape["gz"]
    n_x = min(4, n_gz)
    places = (2, n_gx // 4, 2, n_gz // n_x, n_x)
    in_specs = (P(None, None, "gz", "gx"), P("gx"), P(), P())
    out_specs = (P(None, None, "gz", "gx"), P(None, None, "gz", "gx"), P())
    return jax.shard_map(
        functools.partial(on_device, places),
        mesh=mesh, in_specs=in_specs, out_specs=out_specs, check_vma=False,
    )
```

```python
import functools

import jax
import jax.numpy as jnp
import numpy as np
from jax import lax
from jax.experimental import pallas as pl
from jax.experimental.pallas import tpu as pltpu
from jax.sharding import PartitionSpec as P


MESH = pl.DeviceIdType.MESH
LANES = 128
WEIGHTS = (
    (1.0 / 3.0, (-1.0 / 36.0, -7.0 / 9.0, 0.0, 7.0 / 9.0, 1.0 / 36.0)),
    (2.0 / 11.0, (3.0 / 44.0, 12.0 / 11.0, -102.0 / 44.0, 12.0 / 11.0, 3.0 / 44.0)),
)


def constants():
    point = np.arange(LANES, dtype=np.float64)
    own, arrived = [], []
    leave = np.zeros((8, LANES))
    for which, (alpha, weights) in enumerate(WEIGHTS):
        ratio = (1.0 - np.sqrt(1.0 - 4.0 * alpha * alpha)) / (2.0 * alpha)
        factor = ratio / alpha / (1.0 - ratio * ratio)
        green = lambda d: factor * (-ratio) ** np.abs(d)
        kernel = lambda d: sum(w * green(d + k) for k, w in zip((-2, -1, 0, 1, 2), weights))
        own.append(kernel(point[None, :] - point[:, None]))
        rows = np.zeros((8, LANES))
        for side, sign in ((0, 1.0), (4, -1.0)):
            tail = kernel(sign * 2.0) / ratio**2
            away = point if side == 0 else LANES - 1 - point
            rows[side + which] = tail * (-ratio) ** (away + 1)
            rows[side + 2] = np.where(away == 0, kernel(sign) + tail * ratio, 0.0)
        arrived.append(rows)
        leave[which] = (-ratio) ** (LANES - 1 - point)
        leave[4 + which] = (-ratio) ** point
    leave[2, LANES - 1] = 1.0
    leave[6, 0] = 1.0
    return np.concatenate(own + arrived + [leave]).astype(np.float32)


def halves(array):
    high = array.astype(jnp.bfloat16)
    low = (array - high.astype(jnp.float32)).astype(jnp.bfloat16)
    return high, low


def kernel(
    places, groups, rows, points,
    x_hbm, const_hbm, index_hbm, jac_hbm, bend_hbm,
    first, second, energy_ref,
    x, const, index, jac_tab, bend_tab, split, edge_t, op, edge_op, squares,
    to_right, to_left, from_left, from_right, from_far, to_middle_r, to_middle_l, middle,
    mine_a, slots_a, mine_b, slots_b,
    ready, x_sem, in_sem, halo_send, halo_recv, far_recv, mid_send, mid_recv, a_send, a_recv, b_send, b_recv,
):
    n_zh, n_y, n_core, n_zl, n_x = places
    n_gx = n_zh * n_y * n_core
    n_z = n_zh * n_zl
    halves_x = n_x // 2
    n_a, n_b = n_y * 2, n_z * n_core * halves_x
    gx, gz = lax.axis_index("gx"), lax.axis_index("gz")
    div, rem = lax.div, lax.rem
    core = rem(gx, n_core)
    y = rem(div(gx, n_core), n_y)
    zh = div(gx, n_core * n_y)
    xx = rem(gz, n_x)
    zl = div(gz, n_x)
    z = zh * n_zl + zl
    x_low = rem(xx, 2)
    in_a = y * 2 + x_low
    in_b = (z * n_core + core) * halves_x + div(xx, 2)

    def turned(place, by, size):
        place = place + by
        return jnp.where(place >= size, place - size, place)

    pair_a = xx + 1 - 2 * x_low
    ys = [(zh * n_y + turned(y, by, n_y)) * n_core + core for by in range(n_y)]
    peers_a = [
        (min(by, n_y - by), across, {"gx": ys[by], "gz": zl * n_x + (pair_a if across else xx)})
        for by in range(n_y) for across in range(2) if by + across
    ]
    zs = [turned(z, by, n_z) for by in range(n_z)]
    zs = [(div(there, n_zl) * n_y + y, rem(there, n_zl) * n_x) for there in zs]
    peers_b = [
        (
            min(by, n_z - by),
            across + other,
            {
                "gx": zs[by][0] * n_core + (1 - core if other else core),
                "gz": zs[by][1] + (n_x - 1 - xx if across else xx),
            },
        )
        for by in range(n_z) for other in range(n_core) for across in range(halves_x) if by + other + across
    ]
    peers_a.sort(key=lambda p: -p[0] - p[1])
    peers_b.sort(key=lambda p: -p[0] - p[1])

    near_y, near_z = max(n_y // 4, 1), max(n_z // 4, 1)
    round_one = [p for p in peers_b if p[0] <= near_z] + [p for p in peers_a if p[0] <= near_y]
    round_two = [p for p in peers_b if p[:2] == (near_z, 0) and n_z >= 4]
    round_two += [p for p in peers_a if p[:2] == (near_y, 0) and n_y >= 4]
    peers_a, peers_b, round_one, round_two = (
        [p[2] for p in peers] for peers in (peers_a, peers_b, round_one, round_two)
    )

    lines = groups * rows
    quarter = n_z // 4
    is_last = jnp.logical_and(y == n_y - 1, core == n_core - 1)
    is_first = jnp.logical_and(y == 0, core == 0)

    def in_z(by, at_last):
        there = turned(z, by % n_z, n_z)
        within = n_y * n_core - 1 if at_last else 0
        return {"gx": div(there, n_zl) * n_y * n_core + within, "gz": rem(there, n_zl) * n_x + xx}

    ahead, behind = in_z(quarter, True), in_z(-quarter, True)
    ahead_first = in_z(quarter, False)

    right = {"gx": rem(gx + 1, n_gx), "gz": gz}
    left = {"gx": rem(gx + n_gx - 1, n_gx), "gz": gz}

    def chunk(g):
        return pl.ds(pl.multiple_of(g * rows, rows), rows)

    def load(g):
        return pltpu.make_async_copy(x_hbm.at[chunk(g)], x.at[chunk(g)], x_sem.at[g])

    smalls = [
        pltpu.make_async_copy(src, dst, in_sem.at[n])
        for n, (src, dst) in enumerate(
            ((const_hbm, const), (index_hbm, index), (jac_hbm, jac_tab), (bend_hbm, bend_tab))
        )
    ]
    for copy in smalls:
        copy.start()
    for g in range(groups):
        load(g).start()

    barrier = pltpu.get_barrier_semaphore()

    def greet(semaphore, peer):
        pl.semaphore_signal(semaphore, inc=1, device_id=peer, device_id_type=MESH)

    @pl.when(is_last)
    def _():
        for peer in (ahead_first, ahead, behind):
            greet(barrier, peer)
        from_right[...] = jnp.zeros_like(from_right)

    @pl.when(is_first)
    def _():
        greet(barrier, behind)
        from_left[...] = jnp.zeros_like(from_left)

    @pl.when(jnp.logical_not(is_last))
    def _():
        greet(barrier, right)

    @pl.when(jnp.logical_not(is_first))
    def _():
        greet(barrier, left)

    for peer in round_one:
        greet(barrier, peer)

    for copy in smalls:
        copy.wait()
    table_rows = jac_tab.shape[1]
    onehot = (
        lax.broadcasted_iota(jnp.int32, (table_rows, LANES), 0) == index[...]
    ).astype(jnp.float32)
    tables = jnp.concatenate(
        [jnp.broadcast_to(jac_tab[...], (8, table_rows)), jnp.broadcast_to(bend_tab[...], (8, table_rows))],
        axis=0,
    )
    metric = jnp.dot(tables, onehot, precision=lax.Precision.HIGHEST)
    inv_jac = 1.0 / metric[0:1]
    bend = metric[8:9]

    def scaled(one, two):
        one = one * inv_jac
        return jnp.concatenate([one, (two - bend * one) * (inv_jac * inv_jac)], axis=1)

    own_op = scaled(const[0:128, :], const[128:256, :])
    arrived_op = scaled(const[256:264, :], const[264:272, :])
    arrived_one = arrived_op[:, :LANES]
    joint = lax.dot_general(
        arrived_one, own_op[:, :LANES], (((1,), (1,)), ((), ())),
        precision=lax.Precision.HIGHEST, preferred_element_type=jnp.float32,
    )
    for ref, at in ((to_middle_l, 0), (to_middle_r, 4)):
        sums_of, edge_of = arrived_one[at : at + 1], arrived_one[at + 2 : at + 3]
        for row, (product, times) in enumerate(
            ((sums_of * sums_of, 1.0), (sums_of * edge_of, 2.0), (edge_of * edge_of, 1.0))
        ):
            total = jnp.sum(product, axis=1, keepdims=True) * times
            ref[row : row + 1, lines:] = jnp.broadcast_to(total, (1, LANES))
        ref[3:4, lines:] = jnp.zeros((1, LANES), jnp.float32)
    out_rows = const[272:280, :]
    leave_high, leave_low = halves(
        jnp.concatenate(
            [
                out_rows,
                out_rows[0:1], out_rows[2:3], joint[4:5], joint[6:7],
                out_rows[4:5], out_rows[6:7], joint[0:1], joint[2:3],
            ],
            axis=0,
        )
    )
    leave = jnp.concatenate(
        [
            jnp.concatenate([leave_high, leave_high], axis=1),
            jnp.concatenate([leave_low, leave_low], axis=1),
        ],
        axis=0,
    )

    @pl.loop(0, groups)
    def _(g):
        load(g).wait()
        high, low = halves(x[chunk(g), :])
        both = jnp.concatenate([high, low], axis=1)
        split[chunk(g), :] = both
        sums = lax.dot_general(
            leave, both, (((1,), (1,)), ((), ())), preferred_element_type=jnp.float32
        )
        sums = sums[0:16] + sums[16:32]
        to_right[:, chunk(g)] = sums[0:4]
        to_left[:, chunk(g)] = sums[4:8]
        to_middle_r[:, chunk(g)] = sums[8:12]
        to_middle_l[:, chunk(g)] = sums[12:16]

    pl.semaphore_wait(
        barrier, len(round_one) + jnp.where(is_last, 4, 2)
    )
    middle_r = pltpu.make_async_remote_copy(
        to_middle_r, middle.at[0], mid_send, mid_recv.at[0], device_id=ahead, device_id_type=MESH
    )
    middle_l = pltpu.make_async_remote_copy(
        to_middle_l, middle.at[1], mid_send, mid_recv.at[1], device_id=behind, device_id_type=MESH
    )
    halo_r = pltpu.make_async_remote_copy(
        to_right, from_left, halo_send.at[0], halo_recv.at[0], device_id=right, device_id_type=MESH
    )
    halo_l = pltpu.make_async_remote_copy(
        to_left, from_right, halo_send.at[1], halo_recv.at[1], device_id=left, device_id_type=MESH
    )
    far_r = pltpu.make_async_remote_copy(
        to_right, from_far, halo_send.at[0], far_recv, device_id=right, device_id_type=MESH
    )
    far_l = pltpu.make_async_remote_copy(
        to_left, from_far, halo_send.at[1], far_recv, device_id=left, device_id_type=MESH
    )

    @pl.when(is_last)
    def _():
        middle_r.start()
        halo_l.start()
        greet(ready, ahead_first)

    @pl.when(is_first)
    def _():
        middle_l.start()
        halo_r.start()

    is_inner = jnp.logical_not(jnp.logical_or(is_last, is_first))

    @pl.when(is_inner)
    def _():
        halo_r.start()
        halo_l.start()

    for peer in round_two:
        greet(ready, peer)

    op_high, op_low = halves(own_op)
    op[0:128, :] = op_high
    op[128:256, :] = op_low
    edge_high, edge_low = halves(arrived_op)
    edge_op[...] = jnp.concatenate([edge_high, edge_high, edge_low, edge_low], axis=0)

    @pl.loop(0, groups)
    def _(g):
        both = split[chunk(g), :]
        high = op[0:128, :]
        low = op[128:256, :]
        part = jnp.dot(
            both, jnp.concatenate([high, high], axis=0), preferred_element_type=jnp.float32
        ) + jnp.dot(both, jnp.concatenate([low, low], axis=0), preferred_element_type=jnp.float32)
        first[chunk(g), :] = part[:, :LANES]
        second[chunk(g), :] = part[:, LANES:]

    pl.semaphore_wait(ready, len(round_two) + jnp.where(is_first, 1, 0))

    @pl.when(is_last)
    def _():
        far_r.start()

    @pl.when(is_first)
    def _():
        far_l.start()

    @pl.when(jnp.logical_not(is_first))
    def _():
        halo_r.wait_recv()

    @pl.when(jnp.logical_not(is_last))
    def _():
        halo_l.wait_recv()

    def spread(left_edge, right_edge):
        edge = jnp.concatenate([left_edge, right_edge], axis=0)
        high = edge.astype(jnp.bfloat16).astype(jnp.float32)
        low = edge - high
        return jnp.concatenate([high, low, high, low], axis=0).T.astype(jnp.bfloat16)

    squares[...] = jnp.zeros_like(squares)

    @pl.loop(0, groups)
    def _(g):
        edge = spread(from_left[:, chunk(g)], from_right[:, chunk(g)])
        edge_t[chunk(g), :] = edge
        more = jnp.dot(edge, edge_op[:, :LANES], preferred_element_type=jnp.float32)
        one = first[chunk(g), :] + more
        first[chunk(g), :] = one
        squares[pl.ds(g, 1), :] = jnp.sum(one * one, axis=0, keepdims=True)

    @pl.when(is_last)
    def _():
        middle_r.wait_recv()
        middle_l.wait_recv()
        whole = pl.ds(0, lines)
        right_sum, right_edge = middle[0, 0:1, whole], middle[0, 1:2, whole]
        left_sum, left_edge = middle[1, 0:1, whole], middle[1, 1:2, whole]

        def again(side, row):
            return jnp.concatenate([middle[side, row : row + 1, lines:]] * (lines // LANES), axis=1)

        cross = 2.0 * (
            right_sum * middle[1, 2:3, whole] + right_edge * middle[1, 3:4, whole]
            + left_sum * middle[0, 2:3, whole] + left_edge * middle[0, 3:4, whole]
        )
        for side, some, edge in ((1, right_sum, right_edge), (0, left_sum, left_edge)):
            cross += some * (again(side, 0) * some + again(side, 1) * edge) + again(side, 2) * edge * edge
        for g in range(groups):
            total = squares[g : g + 1, :]
            for at in range(g * rows, (g + 1) * rows, LANES):
                total += cross[:, at : at + LANES]
            squares[g : g + 1, :] = total

    def send(here, mine, slots, peers, send_sem, recv_sem):
        for peer in peers:
            pltpu.make_async_remote_copy(
                mine, slots.at[here], send_sem, recv_sem, device_id=peer, device_id_type=MESH
            ).start()

    def collect(n, slots, send_sem, recv_sem):
        rest = slots.at[pl.ds(0, n - 1)]
        pltpu.make_async_copy(rest, rest, recv_sem).wait()
        pltpu.make_async_copy(rest, rest, send_sem).wait()

    diagonal = lax.broadcasted_iota(jnp.int32, (8, LANES), 0) == lax.broadcasted_iota(
        jnp.int32, (8, LANES), 1
    )
    energy = jnp.sum(squares[...], axis=1, keepdims=True)
    energy = jnp.sum(jnp.where(diagonal, energy, 0.0), axis=0, keepdims=True)
    mine_a[...] = energy
    slots_a[in_a] = energy
    send(in_a, mine_a, slots_a, peers_a, a_send, a_recv)

    @pl.loop(0, groups)
    def _(g):
        more = jnp.dot(edge_t[chunk(g), :], edge_op[:, LANES:], preferred_element_type=jnp.float32)
        second[chunk(g), :] = second[chunk(g), :] + more

    @pl.when(jnp.logical_not(is_inner))
    def _():
        far_r.wait_recv()

        @pl.loop(0, groups)
        def _(g):
            far = from_far[:, chunk(g)]
            edge = spread(jnp.where(is_first, far, 0.0), jnp.where(is_last, far, 0.0))
            more = jnp.dot(edge, edge_op[...], preferred_element_type=jnp.float32)
            first[chunk(g), :] = first[chunk(g), :] + more[:, :LANES]
            second[chunk(g), :] = second[chunk(g), :] + more[:, LANES:]

    collect(n_a, slots_a, a_send, a_recv)
    energy = jnp.sum(slots_a[...], axis=0)
    mine_b[...] = energy
    slots_b[in_b] = energy
    send(in_b, mine_b, slots_b, peers_b, b_send, b_recv)
    collect(n_b, slots_b, b_send, b_recv)
    energy_ref[...] = jnp.sum(slots_b[...], axis=0) * (1.0 / points)
    halo_r.wait_send()
    halo_l.wait_send()

    @pl.when(jnp.logical_not(is_inner))
    def _():
        middle_r.wait_send()


def store(first, second, energy_ref, first_hbm, second_hbm, out_ref, sems):
    lines, pieces = first.shape[0], sems.shape[1]
    step = lines // pieces
    outs = [
        pltpu.make_async_copy(src.at[pl.ds(n * step, step)], dst.at[pl.ds(n * step, step)], sems.at[side, n])
        for n in range(pieces)
        for side, (src, dst) in enumerate(((first, first_hbm), (second, second_hbm)))
    ]
    for copy in outs:
        copy.start()
    planes, comps = out_ref.shape
    energy = energy_ref[...]
    for row in range(planes):
        for col in range(comps):
            at = col * planes + row
            out_ref[row : row + 1, col : col + 1] = energy[:, at : at + 1]
    for copy in outs:
        copy.wait()


def on_device(places, velocity, metric_index, jac_table, bend_table):
    n_zh, n_y, n_core, n_zl, n_x = places
    comps, planes, rows, lanes = velocity.shape
    groups = comps * planes
    lines = groups * rows
    table_rows = jac_table.shape[0]
    points = rows * n_zl * n_x * lanes * n_zh * n_y * n_core
    n_a, n_b = n_y * 2, n_zh * n_zl * n_core * (n_x // 2)
    f32, bf16 = jnp.float32, jnp.bfloat16
    const = jnp.asarray(constants())
    anywhere = pl.BlockSpec(memory_space=pl.ANY)
    vmem = pl.BlockSpec(memory_space=pltpu.VMEM)
    dma = pltpu.SemaphoreType.DMA
    first, second, energy = pl.pallas_call(
        functools.partial(kernel, places, groups, rows, points),
        out_shape=(
            pltpu.VMEM((lines, lanes), f32),
            pltpu.VMEM((lines, lanes), f32),
            pltpu.VMEM((1, lanes), f32),
        ),
        in_specs=[anywhere] * 5,
        out_specs=(vmem, vmem, vmem),
        scratch_shapes=[
            pltpu.VMEM((lines, lanes), f32),
            pltpu.VMEM(const.shape, f32),
            pltpu.VMEM((1, lanes), jnp.int32),
            pltpu.VMEM((1, table_rows), f32),
            pltpu.VMEM((1, table_rows), f32),
            pltpu.VMEM((lines, 2 * lanes), bf16),
            pltpu.VMEM((lines, 32), bf16),
            pltpu.VMEM((2 * lanes, 2 * lanes), bf16),
            pltpu.VMEM((32, 2 * lanes), bf16),
            pltpu.VMEM((8, lanes), f32),
            pltpu.VMEM((4, lines), f32),
            pltpu.VMEM((4, lines), f32),
            pltpu.VMEM((4, lines), f32),
            pltpu.VMEM((4, lines), f32),
            pltpu.VMEM((4, lines), f32),
            pltpu.VMEM((4, lines + lanes), f32),
            pltpu.VMEM((4, lines + lanes), f32),
            pltpu.VMEM((2, 4, lines + lanes), f32),
            pltpu.VMEM((1, lanes), f32),
            pltpu.VMEM((n_a, 1, lanes), f32),
            pltpu.VMEM((1, lanes), f32),
            pltpu.VMEM((n_b, 1, lanes), f32),
            pltpu.SemaphoreType.REGULAR,
            dma((groups,)),
            dma((4,)),
            dma((2,)),
            dma((2,)),
            dma,
            dma,
            dma((2,)),
            dma, dma, dma, dma,
        ],
        compiler_params=pltpu.CompilerParams(collective_id=0, has_side_effects=True),
    )(
        velocity.reshape(lines, lanes),
        const,
        metric_index.reshape(1, lanes),
        jac_table.reshape(1, table_rows),
        bend_table.reshape(1, table_rows),
    )
    whole = jax.ShapeDtypeStruct((lines, lanes), f32)
    first, second, energy = pl.pallas_call(
        store,
        out_shape=(whole, whole, jax.ShapeDtypeStruct((planes, comps), f32)),
        in_specs=[vmem] * 3,
        out_specs=(anywhere, anywhere, vmem),
        scratch_shapes=[dma((2, groups))],
    )(*(pltpu.with_memory_space_constraint(a, pltpu.VMEM) for a in (first, second, energy)))
    return (first.reshape(velocity.shape), second.reshape(velocity.shape), energy.T)


def solution(mesh):
    n_gx, n_gz = mesh.shape["gx"], mesh.shape["gz"]
    n_x = min(4, n_gz)
    places = (2, n_gx // 4, 2, n_gz // n_x, n_x)
    in_specs = (P(None, None, "gz", "gx"), P("gx"), P(), P())
    out_specs = (P(None, None, "gz", "gx"), P(None, None, "gz", "gx"), P())
    return jax.shard_map(
        functools.partial(on_device, places),
        mesh=mesh, in_specs=in_specs, out_specs=out_specs, check_vma=False,
    )
```

```python
import functools

import jax
import jax.numpy as jnp
import numpy as np
from jax import lax
from jax.experimental import pallas as pl
from jax.experimental.pallas import tpu as pltpu
from jax.sharding import PartitionSpec as P


MESH = pl.DeviceIdType.MESH
LANES = 128
WEIGHTS = (
    (1.0 / 3.0, (-1.0 / 36.0, -7.0 / 9.0, 0.0, 7.0 / 9.0, 1.0 / 36.0)),
    (2.0 / 11.0, (3.0 / 44.0, 12.0 / 11.0, -102.0 / 44.0, 12.0 / 11.0, 3.0 / 44.0)),
)


def constants():
    point = np.arange(LANES, dtype=np.float64)
    own, arrived = [], []
    leave = np.zeros((8, LANES))
    for which, (alpha, weights) in enumerate(WEIGHTS):
        ratio = (1.0 - np.sqrt(1.0 - 4.0 * alpha * alpha)) / (2.0 * alpha)
        factor = ratio / alpha / (1.0 - ratio * ratio)
        green = lambda d: factor * (-ratio) ** np.abs(d)
        kernel = lambda d: sum(w * green(d + k) for k, w in zip((-2, -1, 0, 1, 2), weights))
        own.append(kernel(point[None, :] - point[:, None]))
        rows = np.zeros((8, LANES))
        for side, sign in ((0, 1.0), (4, -1.0)):
            tail = kernel(sign * 2.0) / ratio**2
            away = point if side == 0 else LANES - 1 - point
            rows[side + which] = tail * (-ratio) ** (away + 1)
            rows[side + 2] = np.where(away == 0, kernel(sign) + tail * ratio, 0.0)
        arrived.append(rows)
        leave[which] = (-ratio) ** (LANES - 1 - point)
        leave[4 + which] = (-ratio) ** point
    leave[2, LANES - 1] = 1.0
    leave[6, 0] = 1.0
    return np.concatenate(own + arrived + [leave]).astype(np.float32)


def halves(array):
    high = array.astype(jnp.bfloat16)
    low = (array - high.astype(jnp.float32)).astype(jnp.bfloat16)
    return high, low


def kernel(
    places, groups, rows, points,
    x_hbm, const_hbm, index_hbm, jac_hbm, bend_hbm,
    first, second, energy_ref,
    x, const, index, jac_tab, bend_tab, split, edge_t, op, edge_op, squares,
    to_right, to_left, from_left, from_right, from_far, to_middle_r, to_middle_l, middle,
    mine_a, slots_a, mine_b, slots_b,
    ready, x_sem, in_sem, halo_send, halo_recv, far_recv, mid_send, mid_recv, a_send, a_recv, b_send, b_recv,
):
    n_zh, n_y, n_core, n_zl, n_x = places
    n_gx = n_zh * n_y * n_core
    n_z = n_zh * n_zl
    halves_x = n_x // 2
    n_a, n_b = n_y * 2, n_z * n_core * halves_x
    gx, gz = lax.axis_index("gx"), lax.axis_index("gz")
    div, rem = lax.div, lax.rem
    core = rem(gx, n_core)
    y = rem(div(gx, n_core), n_y)
    zh = div(gx, n_core * n_y)
    xx = rem(gz, n_x)
    zl = div(gz, n_x)
    z = zh * n_zl + zl
    x_low = rem(xx, 2)
    in_a = y * 2 + x_low
    in_b = (z * n_core + core) * halves_x + div(xx, 2)

    def turned(place, by, size):
        place = place + by
        return jnp.where(place >= size, place - size, place)

    pair_a = xx + 1 - 2 * x_low
    ys = [(zh * n_y + turned(y, by, n_y)) * n_core + core for by in range(n_y)]
    peers_a = [
        (min(by, n_y - by), across, {"gx": ys[by], "gz": zl * n_x + (pair_a if across else xx)})
        for by in range(n_y) for across in range(2) if by + across
    ]
    zs = [turned(z, by, n_z) for by in range(n_z)]
    zs = [(div(there, n_zl) * n_y + y, rem(there, n_zl) * n_x) for there in zs]
    peers_b = [
        (
            min(by, n_z - by),
            across + other,
            {
                "gx": zs[by][0] * n_core + (1 - core if other else core),
                "gz": zs[by][1] + (n_x - 1 - xx if across else xx),
            },
        )
        for by in range(n_z) for other in range(n_core) for across in range(halves_x) if by + other + across
    ]
    peers_a.sort(key=lambda p: -p[0] - p[1])
    peers_b.sort(key=lambda p: -p[0] - p[1])

    near_y, near_z = max(n_y // 4, 1), max(n_z // 4, 1)
    round_one = [p for p in peers_b if p[0] <= near_z] + [p for p in peers_a if p[0] <= near_y]
    round_two = [p for p in peers_b if p[:2] == (near_z, 0) and n_z >= 4]
    round_two += [p for p in peers_a if p[:2] == (near_y, 0) and n_y >= 4]
    peers_a, peers_b, round_one, round_two = (
        [p[2] for p in peers] for peers in (peers_a, peers_b, round_one, round_two)
    )

    lines = groups * rows
    quarter = n_z // 4
    is_last = jnp.logical_and(y == n_y - 1, core == n_core - 1)
    is_first = jnp.logical_and(y == 0, core == 0)

    def in_z(by, at_last):
        there = turned(z, by % n_z, n_z)
        within = n_y * n_core - 1 if at_last else 0
        return {"gx": div(there, n_zl) * n_y * n_core + within, "gz": rem(there, n_zl) * n_x + xx}

    ahead, behind = in_z(quarter, True), in_z(-quarter, True)
    ahead_first = in_z(quarter, False)

    right = {"gx": rem(gx + 1, n_gx), "gz": gz}
    left = {"gx": rem(gx + n_gx - 1, n_gx), "gz": gz}

    def chunk(g):
        return pl.ds(pl.multiple_of(g * rows, rows), rows)

    def load(g):
        return pltpu.make_async_copy(x_hbm.at[chunk(g)], x.at[chunk(g)], x_sem.at[g])

    smalls = [
        pltpu.make_async_copy(src, dst, in_sem.at[n])
        for n, (src, dst) in enumerate(
            ((const_hbm, const), (index_hbm, index), (jac_hbm, jac_tab), (bend_hbm, bend_tab))
        )
    ]
    for copy in smalls:
        copy.start()
    for g in range(groups):
        load(g).start()

    barrier = pltpu.get_barrier_semaphore()

    def greet(semaphore, peer):
        pl.semaphore_signal(semaphore, inc=1, device_id=peer, device_id_type=MESH)

    @pl.when(is_last)
    def _():
        for peer in (ahead_first, ahead, behind):
            greet(barrier, peer)
        from_right[...] = jnp.zeros_like(from_right)

    @pl.when(is_first)
    def _():
        greet(barrier, behind)
        from_left[...] = jnp.zeros_like(from_left)

    @pl.when(jnp.logical_not(is_last))
    def _():
        greet(barrier, right)

    @pl.when(jnp.logical_not(is_first))
    def _():
        greet(barrier, left)

    for peer in round_one:
        greet(barrier, peer)

    for copy in smalls:
        copy.wait()
    table_rows = jac_tab.shape[1]
    onehot = (
        lax.broadcasted_iota(jnp.int32, (table_rows, LANES), 0) == index[...]
    ).astype(jnp.float32)
    tables = jnp.concatenate(
        [jnp.broadcast_to(jac_tab[...], (8, table_rows)), jnp.broadcast_to(bend_tab[...], (8, table_rows))],
        axis=0,
    )
    metric = jnp.dot(tables, onehot, precision=lax.Precision.HIGHEST)
    inv_jac = 1.0 / metric[0:1]
    bend = metric[8:9]

    def scaled(one, two):
        one = one * inv_jac
        return jnp.concatenate([one, (two - bend * one) * (inv_jac * inv_jac)], axis=1)

    own_op = scaled(const[0:128, :], const[128:256, :])
    arrived_op = scaled(const[256:264, :], const[264:272, :])
    arrived_one = arrived_op[:, :LANES]
    joint = lax.dot_general(
        arrived_one, own_op[:, :LANES], (((1,), (1,)), ((), ())),
        precision=lax.Precision.HIGHEST, preferred_element_type=jnp.float32,
    )
    for ref, at in ((to_middle_l, 0), (to_middle_r, 4)):
        sums_of, edge_of = arrived_one[at : at + 1], arrived_one[at + 2 : at + 3]
        for row, (product, times) in enumerate(
            ((sums_of * sums_of, 1.0), (sums_of * edge_of, 2.0), (edge_of * edge_of, 1.0))
        ):
            total = jnp.sum(product, axis=1, keepdims=True) * times
            ref[row : row + 1, lines:] = jnp.broadcast_to(total, (1, LANES))
        ref[3:4, lines:] = jnp.zeros((1, LANES), jnp.float32)
    out_rows = const[272:280, :]
    leave_high, leave_low = halves(
        jnp.concatenate(
            [
                out_rows,
                out_rows[0:1], out_rows[2:3], joint[4:5], joint[6:7],
                out_rows[4:5], out_rows[6:7], joint[0:1], joint[2:3],
            ],
            axis=0,
        )
    )
    leave = jnp.concatenate(
        [
            jnp.concatenate([leave_high, leave_high], axis=1),
            jnp.concatenate([leave_low, leave_low], axis=1),
        ],
        axis=0,
    )

    @pl.loop(0, groups)
    def _(g):
        load(g).wait()
        high, low = halves(x[chunk(g), :])
        both = jnp.concatenate([high, low], axis=1)
        split[chunk(g), :] = both
        sums = lax.dot_general(
            leave, both, (((1,), (1,)), ((), ())), preferred_element_type=jnp.float32
        )
        sums = sums[0:16] + sums[16:32]
        to_right[:, chunk(g)] = sums[0:4]
        to_left[:, chunk(g)] = sums[4:8]
        to_middle_r[:, chunk(g)] = sums[8:12]
        to_middle_l[:, chunk(g)] = sums[12:16]

    pl.semaphore_wait(
        barrier, len(round_one) + jnp.where(is_last, 4, 2)
    )
    middle_r = pltpu.make_async_remote_copy(
        to_middle_r, middle.at[0], mid_send, mid_recv.at[0], device_id=ahead, device_id_type=MESH
    )
    middle_l = pltpu.make_async_remote_copy(
        to_middle_l, middle.at[1], mid_send, mid_recv.at[1], device_id=behind, device_id_type=MESH
    )
    halo_r = pltpu.make_async_remote_copy(
        to_right, from_left, halo_send.at[0], halo_recv.at[0], device_id=right, device_id_type=MESH
    )
    halo_l = pltpu.make_async_remote_copy(
        to_left, from_right, halo_send.at[1], halo_recv.at[1], device_id=left, device_id_type=MESH
    )
    far_r = pltpu.make_async_remote_copy(
        to_right, from_far, halo_send.at[0], far_recv, device_id=right, device_id_type=MESH
    )
    far_l = pltpu.make_async_remote_copy(
        to_left, from_far, halo_send.at[1], far_recv, device_id=left, device_id_type=MESH
    )

    @pl.when(is_last)
    def _():
        middle_r.start()
        halo_l.start()
        greet(ready, ahead_first)

    @pl.when(is_first)
    def _():
        middle_l.start()
        halo_r.start()

    is_inner = jnp.logical_not(jnp.logical_or(is_last, is_first))

    @pl.when(is_inner)
    def _():
        halo_r.start()
        halo_l.start()

    for peer in round_two:
        greet(ready, peer)

    op_high, op_low = halves(own_op)
    op[0:128, :] = op_high
    op[128:256, :] = op_low
    edge_high, edge_low = halves(arrived_op)
    edge_op[...] = jnp.concatenate([edge_high, edge_high, edge_low, edge_low], axis=0)

    @pl.loop(0, groups)
    def _(g):
        both = split[chunk(g), :]
        high = op[0:128, :]
        low = op[128:256, :]
        part = jnp.dot(
            both, jnp.concatenate([high, high], axis=0), preferred_element_type=jnp.float32
        ) + jnp.dot(both, jnp.concatenate([low, low], axis=0), preferred_element_type=jnp.float32)
        first[chunk(g), :] = part[:, :LANES]
        second[chunk(g), :] = part[:, LANES:]

    pl.semaphore_wait(ready, len(round_two) + jnp.where(is_first, 1, 0))

    @pl.when(is_last)
    def _():
        far_r.start()

    @pl.when(is_first)
    def _():
        far_l.start()

    @pl.when(jnp.logical_not(is_first))
    def _():
        halo_r.wait_recv()

    @pl.when(jnp.logical_not(is_last))
    def _():
        halo_l.wait_recv()

    def spread(left_edge, right_edge):
        edge = jnp.concatenate([left_edge, right_edge], axis=0)
        high = edge.astype(jnp.bfloat16).astype(jnp.float32)
        low = edge - high
        return jnp.concatenate([high, low, high, low], axis=0).T.astype(jnp.bfloat16)

    squares[...] = jnp.zeros_like(squares)

    @pl.loop(0, groups)
    def _(g):
        edge = spread(from_left[:, chunk(g)], from_right[:, chunk(g)])
        edge_t[chunk(g), :] = edge
        more = jnp.dot(edge, edge_op[:, :LANES], preferred_element_type=jnp.float32)
        one = first[chunk(g), :] + more
        first[chunk(g), :] = one
        squares[pl.ds(g, 1), :] = jnp.sum(one * one, axis=0, keepdims=True)

    @pl.when(is_last)
    def _():
        middle_r.wait_recv()
        middle_l.wait_recv()
        whole = pl.ds(0, lines)
        right_sum, right_edge = middle[0, 0:1, whole], middle[0, 1:2, whole]
        left_sum, left_edge = middle[1, 0:1, whole], middle[1, 1:2, whole]

        def again(side, row):
            return jnp.concatenate([middle[side, row : row + 1, lines:]] * (lines // LANES), axis=1)

        cross = 2.0 * (
            right_sum * middle[1, 2:3, whole] + right_edge * middle[1, 3:4, whole]
            + left_sum * middle[0, 2:3, whole] + left_edge * middle[0, 3:4, whole]
        )
        for side, some, edge in ((1, right_sum, right_edge), (0, left_sum, left_edge)):
            cross += some * (again(side, 0) * some + again(side, 1) * edge) + again(side, 2) * edge * edge
        for g in range(groups):
            total = squares[g : g + 1, :]
            for at in range(g * rows, (g + 1) * rows, LANES):
                total += cross[:, at : at + LANES]
            squares[g : g + 1, :] = total

    def send(here, mine, slots, peers, send_sem, recv_sem):
        for peer in peers:
            pltpu.make_async_remote_copy(
                mine, slots.at[here], send_sem, recv_sem, device_id=peer, device_id_type=MESH
            ).start()

    def collect(n, slots, send_sem, recv_sem):
        rest = slots.at[pl.ds(0, n - 1)]
        pltpu.make_async_copy(rest, rest, recv_sem).wait()
        pltpu.make_async_copy(rest, rest, send_sem).wait()

    planes, comps = energy_ref.shape
    row = lax.broadcasted_iota(jnp.int32, (8, LANES), 0)
    lane = lax.broadcasted_iota(jnp.int32, (8, LANES), 1)
    energy = jnp.sum(squares[...], axis=1, keepdims=True)
    energy = jnp.concatenate(
        [
            jnp.sum(jnp.where(row == lane * planes + plane, energy, 0.0), axis=0, keepdims=True)
            for plane in range(planes)
        ],
        axis=0,
    )
    mine_a[...] = energy
    slots_a[in_a] = energy
    send(in_a, mine_a, slots_a, peers_a, a_send, a_recv)

    @pl.loop(0, groups)
    def _(g):
        more = jnp.dot(edge_t[chunk(g), :], edge_op[:, LANES:], preferred_element_type=jnp.float32)
        second[chunk(g), :] = second[chunk(g), :] + more

    @pl.when(jnp.logical_not(is_inner))
    def _():
        far_r.wait_recv()

        @pl.loop(0, groups)
        def _(g):
            far = from_far[:, chunk(g)]
            edge = spread(jnp.where(is_first, far, 0.0), jnp.where(is_last, far, 0.0))
            more = jnp.dot(edge, edge_op[...], preferred_element_type=jnp.float32)
            first[chunk(g), :] = first[chunk(g), :] + more[:, :LANES]
            second[chunk(g), :] = second[chunk(g), :] + more[:, LANES:]

    collect(n_a, slots_a, a_send, a_recv)
    energy = jnp.sum(slots_a[...], axis=0)
    mine_b[...] = energy
    slots_b[in_b] = energy
    send(in_b, mine_b, slots_b, peers_b, b_send, b_recv)
    collect(n_b, slots_b, b_send, b_recv)
    energy_ref[...] = jnp.sum(slots_b[...], axis=0)[:, :comps] * (1.0 / points)
    halo_r.wait_send()
    halo_l.wait_send()

    @pl.when(jnp.logical_not(is_inner))
    def _():
        middle_r.wait_send()


def store(first, second, energy, first_hbm, second_hbm, energy_hbm, sems):
    pairs = ((first, first_hbm), (second, second_hbm), (energy, energy_hbm))
    outs = [pltpu.make_async_copy(src, dst, sems.at[n]) for n, (src, dst) in enumerate(pairs)]
    for copy in outs:
        copy.start()
    for copy in outs:
        copy.wait()


def on_device(places, velocity, metric_index, jac_table, bend_table):
    n_zh, n_y, n_core, n_zl, n_x = places
    comps, planes, rows, lanes = velocity.shape
    groups = comps * planes
    lines = groups * rows
    table_rows = jac_table.shape[0]
    points = rows * n_zl * n_x * lanes * n_zh * n_y * n_core
    n_a, n_b = n_y * 2, n_zh * n_zl * n_core * (n_x // 2)
    f32, bf16 = jnp.float32, jnp.bfloat16
    const = jnp.asarray(constants())
    anywhere = pl.BlockSpec(memory_space=pl.ANY)
    vmem = pl.BlockSpec(memory_space=pltpu.VMEM)
    dma = pltpu.SemaphoreType.DMA
    first, second, energy = pl.pallas_call(
        functools.partial(kernel, places, groups, rows, points),
        out_shape=(
            pltpu.VMEM((lines, lanes), f32),
            pltpu.VMEM((lines, lanes), f32),
            pltpu.VMEM((planes, comps), f32),
        ),
        in_specs=[anywhere] * 5,
        out_specs=(vmem, vmem, vmem),
        scratch_shapes=[
            pltpu.VMEM((lines, lanes), f32),
            pltpu.VMEM(const.shape, f32),
            pltpu.VMEM((1, lanes), jnp.int32),
            pltpu.VMEM((1, table_rows), f32),
            pltpu.VMEM((1, table_rows), f32),
            pltpu.VMEM((lines, 2 * lanes), bf16),
            pltpu.VMEM((lines, 32), bf16),
            pltpu.VMEM((2 * lanes, 2 * lanes), bf16),
            pltpu.VMEM((32, 2 * lanes), bf16),
            pltpu.VMEM((8, lanes), f32),
            pltpu.VMEM((4, lines), f32),
            pltpu.VMEM((4, lines), f32),
            pltpu.VMEM((4, lines), f32),
            pltpu.VMEM((4, lines), f32),
            pltpu.VMEM((4, lines), f32),
            pltpu.VMEM((4, lines + lanes), f32),
            pltpu.VMEM((4, lines + lanes), f32),
            pltpu.VMEM((2, 4, lines + lanes), f32),
            pltpu.VMEM((planes, lanes), f32),
            pltpu.VMEM((n_a, planes, lanes), f32),
            pltpu.VMEM((planes, lanes), f32),
            pltpu.VMEM((n_b, planes, lanes), f32),
            pltpu.SemaphoreType.REGULAR,
            dma((groups,)),
            dma((4,)),
            dma((2,)),
            dma((2,)),
            dma,
            dma,
            dma((2,)),
            dma, dma, dma, dma,
        ],
        compiler_params=pltpu.CompilerParams(collective_id=0, has_side_effects=True),
    )(
        velocity.reshape(lines, lanes),
        const,
        metric_index.reshape(1, lanes),
        jac_table.reshape(1, table_rows),
        bend_table.reshape(1, table_rows),
    )
    whole = jax.ShapeDtypeStruct((lines, lanes), f32)
    first, second, energy = pl.pallas_call(
        store,
        out_shape=(whole, whole, jax.ShapeDtypeStruct((planes, comps), f32)),
        in_specs=[vmem] * 3,
        out_specs=(anywhere, anywhere, anywhere),
        scratch_shapes=[dma((3,))],
    )(*(pltpu.with_memory_space_constraint(a, pltpu.VMEM) for a in (first, second, energy)))
    return (first.reshape(velocity.shape), second.reshape(velocity.shape), energy.T)


def solution(mesh):
    n_gx, n_gz = mesh.shape["gx"], mesh.shape["gz"]
    n_x = min(4, n_gz)
    places = (2, n_gx // 4, 2, n_gz // n_x, n_x)
    in_specs = (P(None, None, "gz", "gx"), P("gx"), P(), P())
    out_specs = (P(None, None, "gz", "gx"), P(None, None, "gz", "gx"), P())
    return jax.shard_map(
        functools.partial(on_device, places),
        mesh=mesh, in_specs=in_specs, out_specs=out_specs, check_vma=False,
    )
```

```python
import functools

import jax
import jax.numpy as jnp
import numpy as np
from jax import lax
from jax.experimental import pallas as pl
from jax.experimental.pallas import tpu as pltpu
from jax.sharding import PartitionSpec as P


MESH = pl.DeviceIdType.MESH
LANES = 128
WEIGHTS = (
    (1.0 / 3.0, (-1.0 / 36.0, -7.0 / 9.0, 0.0, 7.0 / 9.0, 1.0 / 36.0)),
    (2.0 / 11.0, (3.0 / 44.0, 12.0 / 11.0, -102.0 / 44.0, 12.0 / 11.0, 3.0 / 44.0)),
)


def constants():
    point = np.arange(LANES, dtype=np.float64)
    own, arrived = [], []
    leave = np.zeros((8, LANES))
    for which, (alpha, weights) in enumerate(WEIGHTS):
        ratio = (1.0 - np.sqrt(1.0 - 4.0 * alpha * alpha)) / (2.0 * alpha)
        factor = ratio / alpha / (1.0 - ratio * ratio)
        green = lambda d: factor * (-ratio) ** np.abs(d)
        kernel = lambda d: sum(w * green(d + k) for k, w in zip((-2, -1, 0, 1, 2), weights))
        own.append(kernel(point[None, :] - point[:, None]))
        rows = np.zeros((8, LANES))
        for side, sign in ((0, 1.0), (4, -1.0)):
            tail = kernel(sign * 2.0) / ratio**2
            away = point if side == 0 else LANES - 1 - point
            rows[side + which] = tail * (-ratio) ** (away + 1)
            rows[side + 2] = np.where(away == 0, kernel(sign) + tail * ratio, 0.0)
        arrived.append(rows)
        leave[which] = (-ratio) ** (LANES - 1 - point)
        leave[4 + which] = (-ratio) ** point
    leave[2, LANES - 1] = 1.0
    leave[6, 0] = 1.0
    return np.concatenate(own + arrived + [leave]).astype(np.float32)


def halves(array):
    high = array.astype(jnp.bfloat16)
    low = (array - high.astype(jnp.float32)).astype(jnp.bfloat16)
    return high, low


def kernel(
    places, groups, rows, points,
    x_hbm, const_hbm, index_hbm, jac_hbm, bend_hbm,
    first, second, energy_ref,
    x, const, index, jac_tab, bend_tab, split, edge_t, op, edge_op, squares,
    to_right, to_left, from_left, from_right, from_far, to_middle_r, to_middle_l, middle,
    mine_a, slots_a, mine_b, slots_b,
    ready, x_sem, in_sem, halo_send, halo_recv, far_recv, mid_send, mid_recv, a_send, a_recv, b_send, b_recv,
):
    n_zh, n_y, n_core, n_zl, n_x = places
    n_gx = n_zh * n_y * n_core
    n_z = n_zh * n_zl
    halves_x = n_x // 2
    n_a, n_b = n_y * 2, n_z * n_core * halves_x
    gx, gz = lax.axis_index("gx"), lax.axis_index("gz")
    div, rem = lax.div, lax.rem
    core = rem(gx, n_core)
    y = rem(div(gx, n_core), n_y)
    zh = div(gx, n_core * n_y)
    xx = rem(gz, n_x)
    zl = div(gz, n_x)
    z = zh * n_zl + zl
    x_low = rem(xx, 2)
    in_a = y * 2 + x_low
    in_b = (z * n_core + core) * halves_x + div(xx, 2)

    def turned(place, by, size):
        place = place + by
        return jnp.where(place >= size, place - size, place)

    pair_a = xx + 1 - 2 * x_low
    ys = [(zh * n_y + turned(y, by, n_y)) * n_core + core for by in range(n_y)]
    peers_a = [
        (min(by, n_y - by), across, {"gx": ys[by], "gz": zl * n_x + (pair_a if across else xx)})
        for by in range(n_y) for across in range(2) if by + across
    ]
    zs = [turned(z, by, n_z) for by in range(n_z)]
    zs = [(div(there, n_zl) * n_y + y, rem(there, n_zl) * n_x) for there in zs]
    peers_b = [
        (
            min(by, n_z - by),
            across + other,
            {
                "gx": zs[by][0] * n_core + (1 - core if other else core),
                "gz": zs[by][1] + (n_x - 1 - xx if across else xx),
            },
        )
        for by in range(n_z) for other in range(n_core) for across in range(halves_x) if by + other + across
    ]
    peers_a.sort(key=lambda p: -p[0] - p[1])
    peers_b.sort(key=lambda p: -p[0] - p[1])

    near_y, near_z = max(n_y // 4, 1), max(n_z // 4, 1)
    round_one = [p for p in peers_b if p[0] <= near_z] + [p for p in peers_a if p[0] <= near_y]
    round_two = [p for p in peers_b if p[:2] == (near_z, 0) and n_z >= 4]
    round_two += [p for p in peers_a if p[:2] == (near_y, 0) and n_y >= 4]
    peers_a, peers_b, round_one, round_two = (
        [p[2] for p in peers] for peers in (peers_a, peers_b, round_one, round_two)
    )

    lines = groups * rows
    quarter = n_z // 4
    is_last = jnp.logical_and(y == n_y - 1, core == n_core - 1)
    is_first = jnp.logical_and(y == 0, core == 0)

    def in_z(by, at_last):
        there = turned(z, by % n_z, n_z)
        within = n_y * n_core - 1 if at_last else 0
        return {"gx": div(there, n_zl) * n_y * n_core + within, "gz": rem(there, n_zl) * n_x + xx}

    ahead, behind = in_z(quarter, True), in_z(-quarter, True)
    ahead_first = in_z(quarter, False)

    right = {"gx": rem(gx + 1, n_gx), "gz": gz}
    left = {"gx": rem(gx + n_gx - 1, n_gx), "gz": gz}

    def chunk(g):
        return pl.ds(pl.multiple_of(g * rows, rows), rows)

    def load(g):
        return pltpu.make_async_copy(x_hbm.at[chunk(g)], x.at[chunk(g)], x_sem.at[g])

    smalls = [
        pltpu.make_async_copy(src, dst, in_sem.at[n])
        for n, (src, dst) in enumerate(
            (
                (const_hbm, const), (index_hbm, index.at[0]), (jac_hbm, jac_tab.at[0]), (bend_hbm, bend_tab.at[0])
            )
        )
    ]
    for copy in smalls:
        copy.start()
    for g in range(groups):
        load(g).start()

    barrier = pltpu.get_barrier_semaphore()

    def greet(semaphore, peer):
        pl.semaphore_signal(semaphore, inc=1, device_id=peer, device_id_type=MESH)

    @pl.when(is_last)
    def _():
        for peer in (ahead_first, ahead, behind):
            greet(barrier, peer)
        from_right[...] = jnp.zeros_like(from_right)

    @pl.when(is_first)
    def _():
        greet(barrier, behind)
        from_left[...] = jnp.zeros_like(from_left)

    for peer in round_one:
        greet(barrier, peer)

    @pl.when(jnp.logical_not(is_last))
    def _():
        greet(barrier, right)

    @pl.when(jnp.logical_not(is_first))
    def _():
        greet(barrier, left)

    for copy in smalls:
        copy.wait()
    table_rows = jac_tab.shape[2]
    onehot = (
        lax.broadcasted_iota(jnp.int32, (table_rows, LANES), 0) == index[0]
    ).astype(jnp.float32)
    tables = jnp.concatenate(
        [jnp.broadcast_to(jac_tab[0], (8, table_rows)), jnp.broadcast_to(bend_tab[0], (8, table_rows))],
        axis=0,
    )
    metric = jnp.dot(tables, onehot, precision=lax.Precision.HIGHEST)
    inv_jac = 1.0 / metric[0:1]
    bend = metric[8:9]

    def scaled(one, two):
        one = one * inv_jac
        return jnp.concatenate([one, (two - bend * one) * (inv_jac * inv_jac)], axis=1)

    own_op = scaled(const[0:128, :], const[128:256, :])
    arrived_op = scaled(const[256:264, :], const[264:272, :])
    arrived_one = arrived_op[:, :LANES]
    joint = lax.dot_general(
        arrived_one, own_op[:, :LANES], (((1,), (1,)), ((), ())),
        precision=lax.Precision.HIGHEST, preferred_element_type=jnp.float32,
    )
    for ref, at in ((to_middle_l, 0), (to_middle_r, 4)):
        sums_of, edge_of = arrived_one[at : at + 1], arrived_one[at + 2 : at + 3]
        for row, (product, times) in enumerate(
            ((sums_of * sums_of, 1.0), (sums_of * edge_of, 2.0), (edge_of * edge_of, 1.0))
        ):
            total = jnp.sum(product, axis=1, keepdims=True) * times
            ref[row : row + 1, lines : lines + LANES] = jnp.broadcast_to(total, (1, LANES))
        ref[3:4, lines : lines + LANES] = jnp.zeros((1, LANES), jnp.float32)
    out_rows = const[272:280, :]
    leave_high, leave_low = halves(
        jnp.concatenate(
            [
                out_rows,
                out_rows[0:1], out_rows[2:3], joint[4:5], joint[6:7],
                out_rows[4:5], out_rows[6:7], joint[0:1], joint[2:3],
            ],
            axis=0,
        )
    )
    leave = jnp.concatenate(
        [
            jnp.concatenate([leave_high, leave_high], axis=1),
            jnp.concatenate([leave_low, leave_low], axis=1),
        ],
        axis=0,
    )

    @pl.loop(0, groups)
    def _(g):
        load(g).wait()
        high, low = halves(x[chunk(g), :])
        both = jnp.concatenate([high, low], axis=1)
        split[chunk(g), :] = both
        sums = lax.dot_general(
            leave, both, (((1,), (1,)), ((), ())), preferred_element_type=jnp.float32
        )
        sums = sums[0:16] + sums[16:32]
        to_right[:, chunk(g)] = sums[0:4]
        to_left[:, chunk(g)] = sums[4:8]
        to_middle_r[:, chunk(g)] = sums[8:12]
        to_middle_l[:, chunk(g)] = sums[12:16]

    pl.semaphore_wait(
        barrier, len(round_one) + jnp.where(is_last, 4, 2)
    )
    full, fuller = pl.ds(0, lines), pl.ds(0, lines + LANES)
    middle_r = pltpu.make_async_remote_copy(
        to_middle_r.at[:, fuller], middle.at[0, :, fuller], mid_send, mid_recv.at[0], device_id=ahead, device_id_type=MESH
    )
    middle_l = pltpu.make_async_remote_copy(
        to_middle_l.at[:, fuller], middle.at[1, :, fuller], mid_send, mid_recv.at[1], device_id=behind, device_id_type=MESH
    )
    halo_r = pltpu.make_async_remote_copy(
        to_right.at[:, full], from_left.at[:, full], halo_send.at[0], halo_recv.at[0], device_id=right, device_id_type=MESH
    )
    halo_l = pltpu.make_async_remote_copy(
        to_left.at[:, full], from_right.at[:, full], halo_send.at[1], halo_recv.at[1], device_id=left, device_id_type=MESH
    )
    far_r = pltpu.make_async_remote_copy(
        to_right.at[:, full], from_far.at[:, full], halo_send.at[0], far_recv, device_id=right, device_id_type=MESH
    )
    far_l = pltpu.make_async_remote_copy(
        to_left.at[:, full], from_far.at[:, full], halo_send.at[1], far_recv, device_id=left, device_id_type=MESH
    )

    @pl.when(is_last)
    def _():
        middle_r.start()
        halo_l.start()
        greet(ready, ahead_first)

    @pl.when(is_first)
    def _():
        middle_l.start()
        halo_r.start()

    is_inner = jnp.logical_not(jnp.logical_or(is_last, is_first))

    @pl.when(is_inner)
    def _():
        halo_r.start()
        halo_l.start()

    for peer in round_two:
        greet(ready, peer)

    op_high, op_low = halves(own_op)
    op[0:128, :] = op_high
    op[128:256, :] = op_low
    edge_high, edge_low = halves(arrived_op)
    edge_op[...] = jnp.concatenate([edge_high, edge_high, edge_low, edge_low], axis=0)

    @pl.loop(0, groups)
    def _(g):
        both = split[chunk(g), :]
        high = op[0:128, :]
        low = op[128:256, :]
        part = jnp.dot(
            both, jnp.concatenate([high, high], axis=0), preferred_element_type=jnp.float32
        ) + jnp.dot(both, jnp.concatenate([low, low], axis=0), preferred_element_type=jnp.float32)
        first[chunk(g), :] = part[:, :LANES]
        second[chunk(g), :] = part[:, LANES:]

    pl.semaphore_wait(ready, len(round_two) + jnp.where(is_first, 1, 0))

    @pl.when(is_last)
    def _():
        far_r.start()

    @pl.when(is_first)
    def _():
        far_l.start()

    @pl.when(jnp.logical_not(is_first))
    def _():
        halo_r.wait_recv()

    @pl.when(jnp.logical_not(is_last))
    def _():
        halo_l.wait_recv()

    def spread(left_edge, right_edge):
        edge = jnp.concatenate([left_edge, right_edge], axis=0)
        high = edge.astype(jnp.bfloat16).astype(jnp.float32)
        low = edge - high
        return jnp.concatenate([high, low, high, low], axis=0).T.astype(jnp.bfloat16)

    squares[...] = jnp.zeros_like(squares)

    @pl.loop(0, groups)
    def _(g):
        edge = spread(from_left[:, chunk(g)], from_right[:, chunk(g)])
        edge_t[chunk(g), :] = edge
        more = jnp.dot(edge, edge_op[:, :LANES], preferred_element_type=jnp.float32)
        one = first[chunk(g), :] + more
        first[chunk(g), :] = one
        squares[pl.ds(g, 1), :] = jnp.sum(one * one, axis=0, keepdims=True)

    @pl.when(is_last)
    def _():
        middle_r.wait_recv()
        middle_l.wait_recv()
        whole = pl.ds(0, lines)
        right_sum, right_edge = middle[0, 0:1, whole], middle[0, 1:2, whole]
        left_sum, left_edge = middle[1, 0:1, whole], middle[1, 1:2, whole]

        def again(side, row):
            return jnp.concatenate([middle[side, row : row + 1, lines : lines + LANES]] * (lines // LANES), axis=1)

        cross = 2.0 * (
            right_sum * middle[1, 2:3, whole] + right_edge * middle[1, 3:4, whole]
            + left_sum * middle[0, 2:3, whole] + left_edge * middle[0, 3:4, whole]
        )
        for side, some, edge in ((1, right_sum, right_edge), (0, left_sum, left_edge)):
            cross += some * (again(side, 0) * some + again(side, 1) * edge) + again(side, 2) * edge * edge
        for g in range(groups):
            total = squares[g : g + 1, :]
            for at in range(g * rows, (g + 1) * rows, LANES):
                total += cross[:, at : at + LANES]
            squares[g : g + 1, :] = total

    def send(here, mine, slots, peers, send_sem, recv_sem):
        for peer in peers:
            pltpu.make_async_remote_copy(
                mine.at[0], slots.at[here], send_sem, recv_sem, device_id=peer, device_id_type=MESH
            ).start()

    def collect(n, slots, send_sem, recv_sem):
        rest = slots.at[pl.ds(0, n - 1)]
        pltpu.make_async_copy(rest, rest, recv_sem).wait()
        pltpu.make_async_copy(rest, rest, send_sem).wait()

    planes, comps = energy_ref.shape
    row = lax.broadcasted_iota(jnp.int32, (8, LANES), 0)
    lane = lax.broadcasted_iota(jnp.int32, (8, LANES), 1)
    energy = jnp.sum(squares[...], axis=1, keepdims=True)
    energy = jnp.concatenate(
        [
            jnp.sum(jnp.where(row == lane * planes + plane, energy, 0.0), axis=0, keepdims=True)
            for plane in range(planes)
        ],
        axis=0,
    )
    mine_a[0] = energy
    slots_a[in_a] = energy
    send(in_a, mine_a, slots_a, peers_a, a_send, a_recv)

    @pl.loop(0, groups)
    def _(g):
        more = jnp.dot(edge_t[chunk(g), :], edge_op[:, LANES:], preferred_element_type=jnp.float32)
        second[chunk(g), :] = second[chunk(g), :] + more

    collect(n_a, slots_a, a_send, a_recv)
    energy = jnp.sum(slots_a[0:n_a], axis=0)
    mine_b[0] = energy
    slots_b[in_b] = energy
    send(in_b, mine_b, slots_b, peers_b, b_send, b_recv)
    @pl.when(jnp.logical_not(is_inner))
    def _():
        far_r.wait_recv()

        @pl.loop(0, groups)
        def _(g):
            far = from_far[:, chunk(g)]
            edge = spread(jnp.where(is_first, far, 0.0), jnp.where(is_last, far, 0.0))
            more = jnp.dot(edge, edge_op[...], preferred_element_type=jnp.float32)
            first[chunk(g), :] = first[chunk(g), :] + more[:, :LANES]
            second[chunk(g), :] = second[chunk(g), :] + more[:, LANES:]

    collect(n_b, slots_b, b_send, b_recv)
    energy_ref[...] = jnp.sum(slots_b[0:n_b], axis=0)[:, :comps] * (1.0 / points)
    halo_r.wait_send()
    halo_l.wait_send()

    @pl.when(jnp.logical_not(is_inner))
    def _():
        middle_r.wait_send()


def store(first, second, energy, first_hbm, second_hbm, energy_hbm, sems):
    pairs = ((first, first_hbm), (second, second_hbm), (energy, energy_hbm))
    outs = [pltpu.make_async_copy(src, dst, sems.at[n]) for n, (src, dst) in enumerate(pairs)]
    for copy in outs:
        copy.start()
    for copy in outs:
        copy.wait()


def on_device(places, velocity, metric_index, jac_table, bend_table):
    n_zh, n_y, n_core, n_zl, n_x = places
    comps, planes, rows, lanes = velocity.shape
    groups = comps * planes
    lines = groups * rows
    table_rows = jac_table.shape[0]
    points = rows * n_zl * n_x * lanes * n_zh * n_y * n_core
    n_a, n_b = n_y * 2, n_zh * n_zl * n_core * (n_x // 2)
    f32, bf16 = jnp.float32, jnp.bfloat16
    const = jnp.asarray(constants())
    anywhere = pl.BlockSpec(memory_space=pl.ANY)
    vmem = pl.BlockSpec(memory_space=pltpu.VMEM)
    dma = pltpu.SemaphoreType.DMA
    first, second, energy = pl.pallas_call(
        functools.partial(kernel, places, groups, rows, points),
        out_shape=(
            pltpu.VMEM((lines, lanes), f32),
            pltpu.VMEM((lines, lanes), f32),
            pltpu.VMEM((planes, comps), f32),
        ),
        in_specs=[anywhere] * 5,
        out_specs=(vmem, vmem, vmem),
        scratch_shapes=[
            pltpu.VMEM((lines, lanes), f32),
            pltpu.VMEM(const.shape, f32),
            pltpu.VMEM((8, 1, lanes), jnp.int32),
            pltpu.VMEM((8, 1, table_rows), f32),
            pltpu.VMEM((8, 1, table_rows), f32),
            pltpu.VMEM((lines, 2 * lanes), bf16),
            pltpu.VMEM((lines, 32), bf16),
            pltpu.VMEM((2 * lanes, 2 * lanes), bf16),
            pltpu.VMEM((32, 2 * lanes), bf16),
            pltpu.VMEM((8, lanes), f32),
            pltpu.VMEM((4, lines + lanes), f32),
            pltpu.VMEM((4, lines + lanes), f32),
            pltpu.VMEM((4, lines + lanes), f32),
            pltpu.VMEM((4, lines + lanes), f32),
            pltpu.VMEM((4, lines + lanes), f32),
            pltpu.VMEM((4, lines + 2 * lanes), f32),
            pltpu.VMEM((4, lines + 2 * lanes), f32),
            pltpu.VMEM((2, 4, lines + 2 * lanes), f32),
            pltpu.VMEM((8, planes, lanes), f32),
            pltpu.VMEM((n_a + 8, planes, lanes), f32),
            pltpu.VMEM((8, planes, lanes), f32),
            pltpu.VMEM((n_b + 8, planes, lanes), f32),
            pltpu.SemaphoreType.REGULAR,
            dma((groups,)),
            dma((4,)),
            dma((2,)),
            dma((2,)),
            dma,
            dma,
            dma((2,)),
            dma, dma, dma, dma,
        ],
        compiler_params=pltpu.CompilerParams(collective_id=0, has_side_effects=True),
    )(
        velocity.reshape(lines, lanes),
        const,
        metric_index.reshape(1, lanes),
        jac_table.reshape(1, table_rows),
        bend_table.reshape(1, table_rows),
    )
    whole = jax.ShapeDtypeStruct((lines, lanes), f32)
    first, second, energy = pl.pallas_call(
        store,
        out_shape=(whole, whole, jax.ShapeDtypeStruct((planes, comps), f32)),
        in_specs=[vmem] * 3,
        out_specs=(anywhere, anywhere, anywhere),
        scratch_shapes=[dma((3,))],
    )(*(pltpu.with_memory_space_constraint(a, pltpu.VMEM) for a in (first, second, energy)))
    return (first.reshape(velocity.shape), second.reshape(velocity.shape), energy.T)


def solution(mesh):
    n_gx, n_gz = mesh.shape["gx"], mesh.shape["gz"]
    n_x = min(4, n_gz)
    places = (2, n_gx // 4, 2, n_gz // n_x, n_x)
    in_specs = (P(None, None, "gz", "gx"), P("gx"), P(), P())
    out_specs = (P(None, None, "gz", "gx"), P(None, None, "gz", "gx"), P())
    return jax.shard_map(
        functools.partial(on_device, places),
        mesh=mesh, in_specs=in_specs, out_specs=out_specs, check_vma=False,
    )
```

```python
import functools

import jax
import jax.numpy as jnp
import numpy as np
from jax import lax
from jax.experimental import pallas as pl
from jax.experimental.pallas import tpu as pltpu
from jax.sharding import PartitionSpec as P


MESH = pl.DeviceIdType.MESH
LANES = 128
WEIGHTS = (
    (1.0 / 3.0, (-1.0 / 36.0, -7.0 / 9.0, 0.0, 7.0 / 9.0, 1.0 / 36.0)),
    (2.0 / 11.0, (3.0 / 44.0, 12.0 / 11.0, -102.0 / 44.0, 12.0 / 11.0, 3.0 / 44.0)),
)


def constants():
    point = np.arange(LANES, dtype=np.float64)
    own, arrived = [], []
    leave = np.zeros((8, LANES))
    for which, (alpha, weights) in enumerate(WEIGHTS):
        ratio = (1.0 - np.sqrt(1.0 - 4.0 * alpha * alpha)) / (2.0 * alpha)
        factor = ratio / alpha / (1.0 - ratio * ratio)
        green = lambda d: factor * (-ratio) ** np.abs(d)
        kernel = lambda d: sum(w * green(d + k) for k, w in zip((-2, -1, 0, 1, 2), weights))
        own.append(kernel(point[None, :] - point[:, None]))
        rows = np.zeros((8, LANES))
        for side, sign in ((0, 1.0), (4, -1.0)):
            tail = kernel(sign * 2.0) / ratio**2
            away = point if side == 0 else LANES - 1 - point
            rows[side + which] = tail * (-ratio) ** (away + 1)
            rows[side + 2] = np.where(away == 0, kernel(sign) + tail * ratio, 0.0)
        arrived.append(rows)
        leave[which] = (-ratio) ** (LANES - 1 - point)
        leave[4 + which] = (-ratio) ** point
    leave[2, LANES - 1] = 1.0
    leave[6, 0] = 1.0
    return np.concatenate(own + arrived + [leave]).astype(np.float32)


def halves(array):
    high = array.astype(jnp.bfloat16)
    low = (array - high.astype(jnp.float32)).astype(jnp.bfloat16)
    return high, low


def kernel(
    places, groups, rows, points,
    x_hbm, const_hbm, index_hbm, jac_hbm, bend_hbm,
    first, second, energy_ref,
    x, const, index, jac_tab, bend_tab, split, edge_t, op, edge_op, squares,
    to_right, to_left, from_left, from_right, from_far, to_middle_r, to_middle_l, middle,
    mine_a, slots_a, mine_b, slots_b,
    ready, x_sem, in_sem, halo_send, halo_recv, far_recv, mid_send, mid_recv, a_send, a_recv, b_send, b_recv,
):
    n_zh, n_y, n_core, n_zl, n_x = places
    n_gx = n_zh * n_y * n_core
    n_z = n_zh * n_zl
    halves_x = n_x // 2
    n_a, n_b = n_y * 2, n_z * n_core * halves_x
    gx, gz = lax.axis_index("gx"), lax.axis_index("gz")
    div, rem = lax.div, lax.rem
    core = rem(gx, n_core)
    y = rem(div(gx, n_core), n_y)
    zh = div(gx, n_core * n_y)
    xx = rem(gz, n_x)
    zl = div(gz, n_x)
    z = zh * n_zl + zl
    x_low = rem(xx, 2)
    in_a = y * 2 + x_low
    in_b = (z * n_core + core) * halves_x + div(xx, 2)

    def turned(place, by, size):
        place = place + by
        return jnp.where(place >= size, place - size, place)

    pair_a = xx + 1 - 2 * x_low
    ys = [(zh * n_y + turned(y, by, n_y)) * n_core + core for by in range(n_y)]
    peers_a = [
        (min(by, n_y - by), across, {"gx": ys[by], "gz": zl * n_x + (pair_a if across else xx)})
        for by in range(n_y) for across in range(2) if by + across
    ]
    zs = [turned(z, by, n_z) for by in range(n_z)]
    zs = [(div(there, n_zl) * n_y + y, rem(there, n_zl) * n_x) for there in zs]
    peers_b = [
        (
            min(by, n_z - by),
            across + other,
            {
                "gx": zs[by][0] * n_core + (1 - core if other else core),
                "gz": zs[by][1] + (n_x - 1 - xx if across else xx),
            },
        )
        for by in range(n_z) for other in range(n_core) for across in range(halves_x) if by + other + across
    ]
    peers_a.sort(key=lambda p: -p[0] - p[1])
    peers_b.sort(key=lambda p: -p[0] - p[1])

    near_y, near_z = max(n_y // 4, 1), max(n_z // 4, 1)
    round_one = [p for p in peers_b if p[0] <= near_z] + [p for p in peers_a if p[0] <= near_y]
    round_two = [p for p in peers_b if p[:2] == (near_z, 0) and n_z >= 4]
    round_two += [p for p in peers_a if p[:2] == (near_y, 0) and n_y >= 4]
    peers_a, peers_b, round_one, round_two = (
        [p[2] for p in peers] for peers in (peers_a, peers_b, round_one, round_two)
    )

    lines = groups * rows
    quarter = n_z // 4
    is_last = jnp.logical_and(y == n_y - 1, core == n_core - 1)
    is_first = jnp.logical_and(y == 0, core == 0)

    def in_z(by, at_last):
        there = turned(z, by % n_z, n_z)
        within = n_y * n_core - 1 if at_last else 0
        return {"gx": div(there, n_zl) * n_y * n_core + within, "gz": rem(there, n_zl) * n_x + xx}

    ahead, behind = in_z(quarter, True), in_z(-quarter, True)
    ahead_first = in_z(quarter, False)

    right = {"gx": rem(gx + 1, n_gx), "gz": gz}
    left = {"gx": rem(gx + n_gx - 1, n_gx), "gz": gz}

    def chunk(g):
        return pl.ds(pl.multiple_of(g * rows, rows), rows)

    def load(g):
        return pltpu.make_async_copy(x_hbm.at[chunk(g)], x.at[chunk(g)], x_sem.at[g])

    smalls = [
        pltpu.make_async_copy(src, dst, in_sem.at[n])
        for n, (src, dst) in enumerate(
            (
                (const_hbm, const), (index_hbm, index.at[0]), (jac_hbm, jac_tab.at[0]), (bend_hbm, bend_tab.at[0])
            )
        )
    ]
    for copy in smalls:
        copy.start()
    for g in range(groups):
        load(g).start()

    barrier = pltpu.get_barrier_semaphore()

    def greet(semaphore, peer):
        pl.semaphore_signal(semaphore, inc=1, device_id=peer, device_id_type=MESH)

    @pl.when(is_last)
    def _():
        for peer in (ahead_first, ahead, behind):
            greet(barrier, peer)
        from_right[...] = jnp.zeros_like(from_right)

    @pl.when(is_first)
    def _():
        greet(barrier, behind)
        from_left[...] = jnp.zeros_like(from_left)

    for peer in round_one:
        greet(barrier, peer)

    @pl.when(jnp.logical_not(is_last))
    def _():
        greet(barrier, right)

    @pl.when(jnp.logical_not(is_first))
    def _():
        greet(barrier, left)

    for copy in smalls:
        copy.wait()
    table_rows = jac_tab.shape[2]
    onehot = (
        lax.broadcasted_iota(jnp.int32, (table_rows, LANES), 0) == index[0]
    ).astype(jnp.float32)
    tables = jnp.concatenate(
        [jnp.broadcast_to(jac_tab[0], (8, table_rows)), jnp.broadcast_to(bend_tab[0], (8, table_rows))],
        axis=0,
    )
    metric = jnp.dot(tables, onehot, precision=lax.Precision.HIGHEST)
    inv_jac = 1.0 / metric[0:1]
    bend = metric[8:9]

    def scaled(one, two):
        one = one * inv_jac
        return jnp.concatenate([one, (two - bend * one) * (inv_jac * inv_jac)], axis=1)

    own_op = scaled(const[0:128, :], const[128:256, :])
    arrived_op = scaled(const[256:264, :], const[264:272, :])
    arrived_one = arrived_op[:, :LANES]
    joint = lax.dot_general(
        arrived_one, own_op[:, :LANES], (((1,), (1,)), ((), ())),
        precision=lax.Precision.HIGHEST, preferred_element_type=jnp.float32,
    )
    for ref, at in ((to_middle_l, 0), (to_middle_r, 4)):
        sums_of, edge_of = arrived_one[at : at + 1], arrived_one[at + 2 : at + 3]
        for row, (product, times) in enumerate(
            ((sums_of * sums_of, 1.0), (sums_of * edge_of, 2.0), (edge_of * edge_of, 1.0))
        ):
            total = jnp.sum(product, axis=1, keepdims=True) * times
            ref[row : row + 1, lines : lines + LANES] = jnp.broadcast_to(total, (1, LANES))
        ref[3:4, lines : lines + LANES] = jnp.zeros((1, LANES), jnp.float32)
    out_rows = const[272:280, :]
    leave_high, leave_low = halves(
        jnp.concatenate(
            [
                out_rows,
                out_rows[0:1], out_rows[2:3], joint[4:5], joint[6:7],
                out_rows[4:5], out_rows[6:7], joint[0:1], joint[2:3],
            ],
            axis=0,
        )
    )
    leave = jnp.concatenate(
        [
            jnp.concatenate([leave_high, leave_high], axis=1),
            jnp.concatenate([leave_low, leave_low], axis=1),
        ],
        axis=0,
    )

    @pl.loop(0, groups)
    def _(g):
        load(g).wait()
        high, low = halves(x[chunk(g), :])
        both = jnp.concatenate([high, low], axis=1)
        split[chunk(g), :] = both
        sums = lax.dot_general(
            leave, both, (((1,), (1,)), ((), ())), preferred_element_type=jnp.float32
        )
        sums = sums[0:16] + sums[16:32]
        to_right[:, chunk(g)] = sums[0:4]
        to_left[:, chunk(g)] = sums[4:8]
        to_middle_r[:, chunk(g)] = sums[8:12]
        to_middle_l[:, chunk(g)] = sums[12:16]

    pl.semaphore_wait(
        barrier, len(round_one) + jnp.where(is_last, 4, 2)
    )
    full, fuller = pl.ds(0, lines), pl.ds(0, lines + LANES)
    middle_r = pltpu.make_async_remote_copy(
        to_middle_r.at[:, fuller], middle.at[0, :, fuller], mid_send, mid_recv.at[0], device_id=ahead, device_id_type=MESH
    )
    middle_l = pltpu.make_async_remote_copy(
        to_middle_l.at[:, fuller], middle.at[1, :, fuller], mid_send, mid_recv.at[1], device_id=behind, device_id_type=MESH
    )
    halo_r = pltpu.make_async_remote_copy(
        to_right.at[:, full], from_left.at[:, full], halo_send.at[0], halo_recv.at[0], device_id=right, device_id_type=MESH
    )
    halo_l = pltpu.make_async_remote_copy(
        to_left.at[:, full], from_right.at[:, full], halo_send.at[1], halo_recv.at[1], device_id=left, device_id_type=MESH
    )
    far_r = pltpu.make_async_remote_copy(
        to_right.at[:, full], from_far.at[:, full], halo_send.at[0], far_recv, device_id=right, device_id_type=MESH
    )
    far_l = pltpu.make_async_remote_copy(
        to_left.at[:, full], from_far.at[:, full], halo_send.at[1], far_recv, device_id=left, device_id_type=MESH
    )

    @pl.when(is_last)
    def _():
        middle_r.start()
        halo_l.start()
        greet(ready, ahead_first)

    @pl.when(is_first)
    def _():
        middle_l.start()
        halo_r.start()

    is_inner = jnp.logical_not(jnp.logical_or(is_last, is_first))

    @pl.when(is_inner)
    def _():
        halo_r.start()
        halo_l.start()

    for peer in round_two:
        greet(ready, peer)

    op_high, op_low = halves(own_op)
    op[0:128, :] = op_high
    op[128:256, :] = op_low
    edge_high, edge_low = halves(arrived_op)
    edge_op[...] = jnp.concatenate([edge_high, edge_high, edge_low, edge_low], axis=0)

    @pl.loop(0, groups)
    def _(g):
        both = split[chunk(g), :]
        high = op[0:128, :]
        low = op[128:256, :]
        part = jnp.dot(
            both, jnp.concatenate([high, high], axis=0), preferred_element_type=jnp.float32
        ) + jnp.dot(both, jnp.concatenate([low, low], axis=0), preferred_element_type=jnp.float32)
        first[chunk(g), :] = part[:, :LANES]
        second[chunk(g), :] = part[:, LANES:]

    pl.semaphore_wait(ready, len(round_two) + jnp.where(is_first, 1, 0))

    @pl.when(is_last)
    def _():
        far_r.start()

    @pl.when(is_first)
    def _():
        far_l.start()

    @pl.when(jnp.logical_not(is_first))
    def _():
        halo_r.wait_recv()

    @pl.when(jnp.logical_not(is_last))
    def _():
        halo_l.wait_recv()

    def spread(left_edge, right_edge):
        edge = jnp.concatenate([left_edge, right_edge], axis=0)
        high = edge.astype(jnp.bfloat16).astype(jnp.float32)
        low = edge - high
        return jnp.concatenate([high, low, high, low], axis=0).T.astype(jnp.bfloat16)

    squares[...] = jnp.zeros_like(squares)

    @pl.loop(0, groups)
    def _(g):
        edge = spread(from_left[:, chunk(g)], from_right[:, chunk(g)])
        edge_t[chunk(g), :] = edge
        more = jnp.dot(edge, edge_op[:, :LANES], preferred_element_type=jnp.float32)
        one = first[chunk(g), :] + more
        first[chunk(g), :] = one
        squares[pl.ds(g, 1), :] = jnp.sum(one * one, axis=0, keepdims=True)

    @pl.when(is_last)
    def _():
        middle_r.wait_recv()
        middle_l.wait_recv()
        whole = pl.ds(0, lines)
        right_sum, right_edge = middle[0, 0:1, whole], middle[0, 1:2, whole]
        left_sum, left_edge = middle[1, 0:1, whole], middle[1, 1:2, whole]

        def again(side, row):
            return jnp.concatenate([middle[side, row : row + 1, lines : lines + LANES]] * (lines // LANES), axis=1)

        cross = 2.0 * (
            right_sum * middle[1, 2:3, whole] + right_edge * middle[1, 3:4, whole]
            + left_sum * middle[0, 2:3, whole] + left_edge * middle[0, 3:4, whole]
        )
        for side, some, edge in ((1, right_sum, right_edge), (0, left_sum, left_edge)):
            cross += some * (again(side, 0) * some + again(side, 1) * edge) + again(side, 2) * edge * edge
        for g in range(groups):
            total = squares[g : g + 1, :]
            for at in range(g * rows, (g + 1) * rows, LANES):
                total += cross[:, at : at + LANES]
            squares[g : g + 1, :] = total

    def send(here, mine, slots, peers, send_sem, recv_sem):
        for peer in peers:
            pltpu.make_async_remote_copy(
                mine.at[0], slots.at[here], send_sem, recv_sem, device_id=peer, device_id_type=MESH
            ).start()

    def collect(n, slots, semaphore):
        rest = slots.at[pl.ds(0, n - 1)]
        pltpu.make_async_copy(rest, rest, semaphore).wait()

    planes, comps = energy_ref.shape
    row = lax.broadcasted_iota(jnp.int32, (8, LANES), 0)
    lane = lax.broadcasted_iota(jnp.int32, (8, LANES), 1)
    energy = jnp.sum(squares[...], axis=1, keepdims=True)
    energy = jnp.concatenate(
        [
            jnp.sum(jnp.where(row == lane * planes + plane, energy, 0.0), axis=0, keepdims=True)
            for plane in range(planes)
        ],
        axis=0,
    )
    mine_a[0] = energy
    slots_a[in_a] = energy
    send(in_a, mine_a, slots_a, peers_a, a_send, a_recv)

    @pl.loop(0, groups)
    def _(g):
        more = jnp.dot(edge_t[chunk(g), :], edge_op[:, LANES:], preferred_element_type=jnp.float32)
        second[chunk(g), :] = second[chunk(g), :] + more

    collect(n_a, slots_a, a_recv)
    energy = jnp.sum(slots_a[0:n_a], axis=0)
    mine_b[0] = energy
    slots_b[in_b] = energy
    send(in_b, mine_b, slots_b, peers_b, b_send, b_recv)
    @pl.when(jnp.logical_not(is_inner))
    def _():
        far_r.wait_recv()

        @pl.loop(0, groups)
        def _(g):
            far = from_far[:, chunk(g)]
            edge = spread(jnp.where(is_first, far, 0.0), jnp.where(is_last, far, 0.0))
            more = jnp.dot(edge, edge_op[...], preferred_element_type=jnp.float32)
            first[chunk(g), :] = first[chunk(g), :] + more[:, :LANES]
            second[chunk(g), :] = second[chunk(g), :] + more[:, LANES:]

    collect(n_b, slots_b, b_recv)
    energy_ref[...] = jnp.sum(slots_b[0:n_b], axis=0)[:, :comps] * (1.0 / points)
    collect(n_a, slots_a, a_send)
    collect(n_b, slots_b, b_send)
    halo_r.wait_send()
    halo_l.wait_send()

    @pl.when(jnp.logical_not(is_inner))
    def _():
        middle_r.wait_send()


def store(first, second, energy, first_hbm, second_hbm, energy_hbm, sems):
    pairs = ((first, first_hbm), (second, second_hbm), (energy, energy_hbm))
    outs = [pltpu.make_async_copy(src, dst, sems.at[n]) for n, (src, dst) in enumerate(pairs)]
    for copy in outs:
        copy.start()
    for copy in outs:
        copy.wait()


def on_device(places, velocity, metric_index, jac_table, bend_table):
    n_zh, n_y, n_core, n_zl, n_x = places
    comps, planes, rows, lanes = velocity.shape
    groups = comps * planes
    lines = groups * rows
    table_rows = jac_table.shape[0]
    points = rows * n_zl * n_x * lanes * n_zh * n_y * n_core
    n_a, n_b = n_y * 2, n_zh * n_zl * n_core * (n_x // 2)
    f32, bf16 = jnp.float32, jnp.bfloat16
    const = jnp.asarray(constants())
    anywhere = pl.BlockSpec(memory_space=pl.ANY)
    vmem = pl.BlockSpec(memory_space=pltpu.VMEM)
    dma = pltpu.SemaphoreType.DMA
    first, second, energy = pl.pallas_call(
        functools.partial(kernel, places, groups, rows, points),
        out_shape=(
            pltpu.VMEM((lines, lanes), f32),
            pltpu.VMEM((lines, lanes), f32),
            pltpu.VMEM((planes, comps), f32),
        ),
        in_specs=[anywhere] * 5,
        out_specs=(vmem, vmem, vmem),
        scratch_shapes=[
            pltpu.VMEM((lines, lanes), f32),
            pltpu.VMEM(const.shape, f32),
            pltpu.VMEM((8, 1, lanes), jnp.int32),
            pltpu.VMEM((8, 1, table_rows), f32),
            pltpu.VMEM((8, 1, table_rows), f32),
            pltpu.VMEM((lines, 2 * lanes), bf16),
            pltpu.VMEM((lines, 32), bf16),
            pltpu.VMEM((2 * lanes, 2 * lanes), bf16),
            pltpu.VMEM((32, 2 * lanes), bf16),
            pltpu.VMEM((8, lanes), f32),
            pltpu.VMEM((4, lines + lanes), f32),
            pltpu.VMEM((4, lines + lanes), f32),
            pltpu.VMEM((4, lines + lanes), f32),
            pltpu.VMEM((4, lines + lanes), f32),
            pltpu.VMEM((4, lines + lanes), f32),
            pltpu.VMEM((4, lines + 2 * lanes), f32),
            pltpu.VMEM((4, lines + 2 * lanes), f32),
            pltpu.VMEM((2, 4, lines + 2 * lanes), f32),
            pltpu.VMEM((8, planes, lanes), f32),
            pltpu.VMEM((n_a + 8, planes, lanes), f32),
            pltpu.VMEM((8, planes, lanes), f32),
            pltpu.VMEM((n_b + 8, planes, lanes), f32),
            pltpu.SemaphoreType.REGULAR,
            dma((groups,)),
            dma((4,)),
            dma((2,)),
            dma((2,)),
            dma,
            dma,
            dma((2,)),
            dma, dma, dma, dma,
        ],
        compiler_params=pltpu.CompilerParams(collective_id=0, has_side_effects=True),
    )(
        velocity.reshape(lines, lanes),
        const,
        metric_index.reshape(1, lanes),
        jac_table.reshape(1, table_rows),
        bend_table.reshape(1, table_rows),
    )
    whole = jax.ShapeDtypeStruct((lines, lanes), f32)
    first, second, energy = pl.pallas_call(
        store,
        out_shape=(whole, whole, jax.ShapeDtypeStruct((planes, comps), f32)),
        in_specs=[vmem] * 3,
        out_specs=(anywhere, anywhere, anywhere),
        scratch_shapes=[dma((3,))],
    )(*(pltpu.with_memory_space_constraint(a, pltpu.VMEM) for a in (first, second, energy)))
    return (first.reshape(velocity.shape), second.reshape(velocity.shape), energy.T)


def solution(mesh):
    n_gx, n_gz = mesh.shape["gx"], mesh.shape["gz"]
    n_x = min(4, n_gz)
    places = (2, n_gx // 4, 2, n_gz // n_x, n_x)
    in_specs = (P(None, None, "gz", "gx"), P("gx"), P(), P())
    out_specs = (P(None, None, "gz", "gx"), P(None, None, "gz", "gx"), P())
    return jax.shard_map(
        functools.partial(on_device, places),
        mesh=mesh, in_specs=in_specs, out_specs=out_specs, check_vma=False,
    )
```
